256 devices in a mesh: row: 32 (over z_hi, y, core), col: 8 (over z_lo, x).
Axes of the slice: x: 4, y: 4, z: 8 (z_hi: 4, z_lo: 2; z = z_hi * 2 + z_lo), core: 2. Of those that a mesh axis runs over, the one named last changes fastest.
Arguments:
- known_inverse: float32 [20480, 20480], P('row', 'col'), may hold values from -1.7818667 to 1.7818667, as said below
- first_panel: float32 [20480, 512], P('col', 'row'), may hold values from -1.25 to 1.25
- second_panel: float32 [20480, 512], P('col', 'row'), may hold values from -1.25 to 1.25
- coupling: float32 [512, 512], replicated, may hold values from -0.25 to 0.25
- first_diag: float32 [512, 512], replicated, may hold values from -6 to 6
- second_diag: float32 [512, 512], replicated, may hold values from -6 to 6
- first_present: int32 [160], replicated, may hold values 0 or 1
- second_present: int32 [160], replicated, may hold values 0 or 1
Outputs:
- first_block: float32 [20480, 512], P(('row', 'col'))
- first_inverse_diag: float32 [512, 512], P(None, 'col')
- second_block: float32 [20480, 512], P(('row', 'col'))
- second_cross: float32 [512, 512], P(None, 'col')
- second_inverse_diag: float32 [512, 512], P(None, 'col')
The draws below stay inside these ranges and needn't reach their ends.
Inputs may be any that keep to these rules, and one draw needn't show every extreme that they name: known_inverse is exactly symmetric.
All inputs are finite; a program needn't handle non-finite values.
Results may differ from the reference program's by a relative error of at most 0.000098.
Values sent between devices are 32-bit elements; how exact they have to be, the bound alone decides.
A program may use at most 64 MiB of HBM per device.

```python
import jax
import jax.numpy as jnp
from jax import lax

S = 20480
W = 512
BLK = 128
NB = 160


def draw_known_inverse(key, part):
    first_key = jax.random.fold_in(jax.random.fold_in(key, 11), 0)
    base = jnp.clip(jax.random.normal(first_key, (S, S), jnp.float32), -5.0, 5.0)
    result = (base + base.T) * (4.0 / (2.0 * S) ** 0.5)
    return result


def place_ends(entries, rng, low, top_value):
    dims = entries.shape
    spot = [jax.random.randint(jax.random.fold_in(rng, axis), (), 0, dims[axis]) for axis in range(len(dims))]
    entries = entries.at[tuple(spot)].set(low)
    longest = dims.index(max(dims))
    spot[longest] = (spot[longest] + 1) % dims[longest]
    return entries.at[tuple(spot)].set(top_value)


def levels(stream_key, shape, pieces, smallest, largest):
    loudness = 1.0
    for position, blocks in pieces:
        steps = jax.random.uniform(jax.random.fold_in(jax.random.fold_in(stream_key, 6), position), (blocks,), jnp.float32, smallest / len(pieces), largest / len(pieces))
        loudness = loudness * jnp.repeat(jnp.exp(steps), shape[position] // blocks).reshape((-1,) + (1,) * (len(shape) - 1 - position))
    return loudness


def gaussian(stream_key, extent, deviation, reach, cuts=(), kind=jnp.bfloat16):
    drawn = deviation * jax.random.normal(stream_key, extent, jnp.float32)
    if cuts:
        drawn = drawn * levels(stream_key, extent, cuts, -0.22, 0.18)
    return jnp.clip(drawn, -reach, reach).astype(kind)


def setup_inputs(seed: int = 0) -> dict:
    seeds = jax.random.split(jax.random.key(seed), 9)
    known_inverse = draw_known_inverse(jax.random.fold_in(seeds[8], 71), 0)
    first_panel = gaussian(seeds[1], (S, W), (S ** -0.25), 1.25, ((0, 8), (1, 32)), jnp.float32)
    second_panel = gaussian(seeds[2], (S, W), (S ** -0.25), 1.25, ((0, 8), (1, 32)), jnp.float32)
    coupling = gaussian(seeds[3], (W, W), W ** -0.5, 0.25, (), jnp.float32)
    first_diag = gaussian(seeds[4], (W, W), 1.0, 6.0, (), jnp.float32)
    second_diag = gaussian(seeds[5], (W, W), 1.0, 6.0, (), jnp.float32)
    first_present = place_ends((jax.random.randint(seeds[6], (NB,), 0, 2) < 1).astype(jnp.int32), jax.random.fold_in(seeds[6], 1), 0, 1)
    second_present = place_ends((jax.random.randint(seeds[7], (NB,), 0, 2) < 1).astype(jnp.int32), jax.random.fold_in(seeds[7], 1), 0, 1)
    return {"known_inverse": known_inverse, "first_panel": first_panel, "second_panel": second_panel, "coupling": coupling, "first_diag": first_diag, "second_diag": second_diag, "first_present": first_present, "second_present": second_present}


def product(left, right):
    return jnp.dot(left, right, precision=lax.Precision.HIGHEST, preferred_element_type=jnp.float32)


def present_rows(present):
    return jnp.repeat(present.astype(jnp.float32), BLK)[:, None]


def reference(known_inverse, first_panel, second_panel, coupling, first_diag, second_diag, first_present, second_present):
    panel_one = first_panel * present_rows(first_present)
    panel_two = second_panel * present_rows(second_present)
    first_block = -product(known_inverse, panel_one)
    first_inverse_diag = first_diag - product(panel_one.T, first_block)
    second_block = -(product(known_inverse, panel_two) + product(first_block, coupling))
    second_cross = -(product(first_block.T, panel_two) + product(first_inverse_diag, coupling))
    second_inverse_diag = second_diag - product(panel_two.T, second_block) - product(coupling.T, second_cross)
    return first_block, first_inverse_diag, second_block, second_cross, second_inverse_diag
```

```python
import functools

import jax
import jax.numpy as jnp
from jax import lax
from jax.experimental import pallas as pl
from jax.experimental.pallas import tpu as pltpu
from jax.sharding import PartitionSpec as P

BLK = 128
MESH = pl.DeviceIdType.MESH
F32 = jnp.float32
BF16 = jnp.bfloat16
KSTEP = 512


def split(x):
    hi = x.astype(BF16)
    return hi, (x - hi.astype(F32)).astype(BF16)


def dot3(left, right, dims):
    lh, ll = split(left)
    rh, rl = split(right)
    g = functools.partial(lax.dot_general, dimension_numbers=(dims, ((), ())), preferred_element_type=F32)
    return g(lh, rh) + (g(lh, rl) + g(ll, rh))


class Sends:
    def __init__(self, sems):
        self.sems = sems
        self.started = []

    def __call__(self, src, dst, recv, device):
        copy = pltpu.make_async_remote_copy(
            src_ref=src, dst_ref=dst, send_sem=self.sems.at[len(self.started)], recv_sem=recv,
            device_id=device, device_id_type=MESH,
        )
        copy.start()
        self.started.append(copy)
        return copy

    def finish(self):
        for copy in self.started:
            copy.wait_send()


def panel_kernel(
    k_hbm, one_hbm, two_hbm, coupling, present_one, present_two,
    x1_out, x2_out, p80_out,
    k_f32, k_hi, k_lo, panels, mask, y, from_x, half_out, half_in, own, turned, y_two,
    local_sem, send_sem, recv_sem, x_sem, z_sem, p_send, p_recv,
):
    row = lax.axis_index("row")
    col = lax.axis_index("col")
    g0, y0, k0 = row // 8, (row // 2) % 4, row % 2
    z0, x0 = col // 4, col % 4

    def at(g, yy, k):
        return ((g % 4) * 8 + (yy % 4) * 2 + k, col)

    y_up, y_down = at(g0, y0 + 1, k0), at(g0, y0 + 3, k0)
    g_up, g_down = at(g0 + 1, y0, k0), at(g0 + 3, y0, k0)
    sibling = at(g0, y0, 1 - k0)
    x_mate = [(row, z0 * 4 + (x0 + d) % 4) for d in (1, 2, 3)]
    z_mate = (row, (1 - z0) * 4 + x0)
    p_target = (col * 4 + row // 8, row % 8)
    p_source = ((row % 4) * 8 + col, row // 4)
    stays = jnp.logical_and(p_target[0] == row, p_target[1] == col)

    k_copy = pltpu.make_async_copy(k_hbm, k_f32, local_sem.at[0])
    k_copy.start()
    firsts = [
        pltpu.make_async_copy(one_hbm, panels.at[g0, 0, y0, k0], local_sem.at[1]),
        pltpu.make_async_copy(two_hbm, panels.at[g0, 1, y0, k0], local_sem.at[2]),
    ]
    for copy in firsts:
        copy.start()

    barrier = pltpu.get_barrier_semaphore()
    for device in (y_up, y_down, g_up, g_down, sibling, *x_mate, z_mate):
        pl.semaphore_signal(barrier, inc=1, device_id=device, device_id_type=MESH)

    @pl.when(jnp.logical_not(stays))
    def _():
        pl.semaphore_signal(barrier, inc=1, device_id=p_target, device_id_type=MESH)
        pl.semaphore_signal(barrier, inc=1, device_id=p_source, device_id_type=MESH)

    pl.semaphore_wait(barrier, jnp.where(stays, 9, 11))
    for copy in firsts:
        copy.wait()

    send = Sends(send_sem)

    def part(g, p, yy, k):
        return panels.at[g % 4, p, yy % 4, k]

    def push(g, p, yy, k, device):
        ref = part(g, p, yy, k)
        send(ref, ref, recv_sem.at[g % 4, p, yy % 4, k], device)

    def arrive(g, p, yy, k):
        ref = part(g, p, yy, k)
        pltpu.make_async_remote_copy(
            src_ref=ref, dst_ref=ref, send_sem=send_sem.at[0], recv_sem=recv_sem.at[g % 4, p, yy % 4, k],
            device_id=sibling, device_id_type=MESH,
        ).wait_recv()

    def spread_y(g):
        for p in (0, 1):
            push(g, p, y0, k0, y_up)
            push(g, 1 - p, y0, k0, y_down)
        push(g, 0, y0, k0, sibling)
        push(g, 1, y0, k0, sibling)

    def relay_y(g):
        arrive(g, 0, y0 + 3, k0)
        push(g, 0, y0 + 3, k0, y_up)
        push(g, 0, y0 + 3, k0, sibling)
        arrive(g, 1, y0 + 1, k0)
        push(g, 1, y0 + 1, k0, y_down)
        push(g, 1, y0 + 1, k0, sibling)
        arrive(g, 1, y0 + 3, k0)
        push(g, 1, y0 + 3, k0, sibling)
        arrive(g, 0, y0 + 1, k0)
        push(g, 0, y0 + 1, k0, sibling)

    def end_y(g):
        for p in (0, 1):
            arrive(g, p, y0 + 2, k0)
            push(g, p, y0 + 2, k0, sibling)

    def compute(t, g):
        for yy in range(4):
            for p in (0, 1):
                arrive(g, p, y0 + yy, 1 - k0)
        group = g % 4
        y_ref = y.at[t]

        def step(i, carry):
            lanes = pl.ds(pl.multiple_of(i * KSTEP, KSTEP), KSTEP)
            block = panels[group, :, :, :, :, lanes].reshape(2, 16, 8, KSTEP)
            block = (block * mask[:, :, lanes][:, None]).reshape(256, KSTEP)
            ph, plo = split(block)
            kh, kl = k_hi[:, lanes], k_lo[:, lanes]
            dims = (((1,), (1,)), ((), ()))
            g2 = functools.partial(lax.dot_general, dimension_numbers=dims, preferred_element_type=F32)
            total = (g2(kh, ph) + g2(kl, ph) + g2(kh, plo)).reshape(2, 4, 80, 256)

            @pl.when(i == 0)
            def _():
                y_ref[...] = total

            @pl.when(i > 0)
            def _():
                y_ref[...] += total

            return carry

        lax.fori_loop(0, 2560 // KSTEP, step, 0)
        for d in (1, 2, 3):
            send(y.at[t, :, (x0 + d) % 4], from_x.at[t, d - 1], x_sem.at[t, d - 1], x_mate[d - 1])
        start = jnp.minimum((row * 80) // BLK, 2560 // BLK - 2) * BLK
        lanes = pl.ds(pl.multiple_of(start, BLK), 256)
        window = panels[group, :, :, :, :, lanes].reshape(2, 16, 8, 256)
        window = (window * mask[:, :, lanes][:, None]).reshape(256, 256)
        turned[t] = window.T
        piece = turned.at[t, pl.ds(pl.multiple_of(row * 80 - start, 8), 80)]

        @pl.when(stays)
        def _():
            copy = pltpu.make_async_copy(piece, p80_out.at[group], local_sem.at[3])
            copy.start()
            copy.wait()

        @pl.when(jnp.logical_not(stays))
        def _():
            pltpu.make_async_remote_copy(
                src_ref=piece, dst_ref=p80_out.at[group], send_sem=p_send.at[t], recv_sem=p_recv.at[group],
                device_id=p_target, device_id_type=MESH,
            ).start()

    def reduce_x(t):
        for d in range(3):
            pltpu.make_async_remote_copy(
                src_ref=from_x.at[t, d], dst_ref=from_x.at[t, d], send_sem=send_sem.at[0], recv_sem=x_sem.at[t, d],
                device_id=sibling, device_id_type=MESH,
            ).wait_recv()

        def total(z):
            return y[t, z, x0] + from_x[t, 0, z] + from_x[t, 1, z] + from_x[t, 2, z]

        half_out[t] = total(1 - z0)
        send(half_out.at[t], half_in.at[t], z_sem.at[t], z_mate)
        own[t] = total(z0)

    def finish_y(t, g):
        pltpu.make_async_remote_copy(
            src_ref=half_in.at[t], dst_ref=half_in.at[t], send_sem=send_sem.at[0], recv_sem=z_sem.at[t],
            device_id=sibling, device_id_type=MESH,
        ).wait_recv()
        done = own[t] + half_in[t]
        lanes = pl.ds(pl.multiple_of((g % 4) * BLK, BLK), BLK)
        x1_out[:, lanes] = -done[:, :BLK]
        y_two[:, lanes] = done[:, BLK:]

    order = (g0, g0 + 1, g0 + 3, g0 + 2)

    for p in (0, 1):
        push(g0, p, y0, k0, y_up)
        push(g0, 1 - p, y0, k0, y_down)
        push(g0, p, y0, k0, g_up)
        push(g0, 1 - p, y0, k0, g_down)
        push(g0, p, y0, k0, sibling)

    for p, present in ((0, present_one), (1, present_two)):
        for j in range(2560 // BLK):
            value = present[col * (2560 // BLK) + j].astype(F32)
            mask[p, :, j * BLK:(j + 1) * BLK] = jnp.full((8, BLK), value, F32)
    k_copy.wait()

    def split_rows(i, carry):
        rows = pl.ds(pl.multiple_of(i * 32, 32), 32)
        hi, lo = split(k_f32[rows, :])
        k_hi[rows, :] = hi
        k_lo[rows, :] = lo
        return carry

    lax.fori_loop(0, 20, split_rows, 0)

    relay_y(order[0])
    arrive(g0 + 3, 0, y0, k0)
    push(g0 + 3, 0, y0, k0, g_up)
    arrive(g0 + 1, 1, y0, k0)
    push(g0 + 1, 1, y0, k0, g_down)
    end_y(order[0])
    arrive(g0 + 1, 0, y0, k0)
    spread_y(order[1])
    compute(0, order[0])
    relay_y(order[1])
    arrive(g0 + 3, 1, y0, k0)
    spread_y(order[2])
    end_y(order[1])
    compute(1, order[1])
    reduce_x(0)
    relay_y(order[2])
    arrive(g0 + 2, 0, y0, k0)
    arrive(g0 + 2, 1, y0, k0)
    spread_y(order[3])
    end_y(order[2])
    compute(2, order[2])
    reduce_x(1)
    finish_y(0, order[0])
    relay_y(order[3])
    end_y(order[3])
    compute(3, order[3])
    reduce_x(2)
    finish_y(1, order[1])
    reduce_x(3)
    finish_y(2, order[2])
    finish_y(3, order[3])
    x2_out[...] = -(y_two[...] + dot3(x1_out[...], coupling[...], ((1,), (0,))))

    send.finish()

    @pl.when(jnp.logical_not(stays))
    def _():
        for t in range(4):
            copy = pltpu.make_async_remote_copy(
                src_ref=turned.at[t, pl.ds(0, 80)], dst_ref=p80_out.at[t], send_sem=p_send.at[t],
                recv_sem=p_recv.at[t], device_id=p_target, device_id_type=MESH,
            )
            copy.wait_send()
            copy.wait_recv()


def panel_stage(known_inverse, one, two, coupling, present_one, present_two):
    vmem = pl.BlockSpec(memory_space=pltpu.VMEM)
    hbm = pl.BlockSpec(memory_space=pl.ANY)
    smem = pl.BlockSpec(memory_space=pltpu.SMEM)
    dma = pltpu.SemaphoreType.DMA
    return pl.pallas_call(
        panel_kernel,
        out_shape=(
            jax.ShapeDtypeStruct((80, 512), F32),
            jax.ShapeDtypeStruct((80, 512), F32),
            jax.ShapeDtypeStruct((4, 80, 256), F32),
        ),
        in_specs=[hbm, hbm, hbm, vmem, smem, smem],
        out_specs=(vmem, vmem, vmem),
        scratch_shapes=[
            pltpu.VMEM((640, 2560), F32),
            pltpu.VMEM((640, 2560), BF16),
            pltpu.VMEM((640, 2560), BF16),
            pltpu.VMEM((4, 2, 4, 2, 16, 2560), F32),
            pltpu.VMEM((2, 8, 2560), F32),
            pltpu.VMEM((4, 2, 4, 80, 256), F32),
            pltpu.VMEM((4, 3, 2, 80, 256), F32),
            pltpu.VMEM((4, 80, 256), F32),
            pltpu.VMEM((4, 80, 256), F32),
            pltpu.VMEM((4, 80, 256), F32),
            pltpu.VMEM((4, 256, 256), F32),
            pltpu.VMEM((80, 512), F32),
            dma((4,)),
            dma((82,)),
            dma((4, 2, 4, 2)),
            dma((4, 3)),
            dma((4,)),
            dma((4,)),
            dma((4,)),
        ],
        compiler_params=pltpu.CompilerParams(
            collective_id=0, has_side_effects=True, vmem_limit_bytes=56 * 2**20
        ),
        name="panels",
    )(known_inverse, one, two, coupling, present_one, present_two)


def dot_high(left, right, dims):
    return lax.dot_general(left, right, (dims, ((), ())), precision=lax.Precision.HIGH, preferred_element_type=F32)


def on_device(known_inverse, first_panel, second_panel, coupling, first_diag, second_diag, first_present, second_present):
    x1, x2, p80 = panel_stage(known_inverse, first_panel.T, second_panel.T, coupling, first_present, second_present)
    p = p80.reshape(4, 80, 2, 128).transpose(2, 1, 0, 3).reshape(2, 80, 512)
    rows = ((0,), (0,))
    sums = jnp.stack([dot_high(x1, p[0], rows), dot_high(x2, p[0], rows), dot_high(x2, p[1], rows)], axis=1)
    mine = lax.psum_scatter(sums, "col", scatter_dimension=0, tiled=True)
    mine = lax.psum(mine, "row")
    start = lax.axis_index("col") * 64
    diag_one = lax.dynamic_slice_in_dim(first_diag, start, 64, 1)
    diag_two = lax.dynamic_slice_in_dim(second_diag, start, 64, 1)
    coupling_part = lax.dynamic_slice_in_dim(coupling, start, 64, 1)
    first_out = diag_one - mine[:, 0].T
    cross = -mine[:, 1].T - dot_high(first_diag, coupling_part, ((1,), (0,)))
    second_out = diag_two - mine[:, 2].T - dot_high(coupling, cross, ((0,), (0,)))
    return x1, first_out, x2, cross, second_out


def solution(mesh):
    in_specs = (P("row", "col"), P("col", "row"), P("col", "row"), P(), P(), P(), P(), P())
    out_specs = (P(("row", "col"), None), P(None, "col"), P(("row", "col"), None), P(None, "col"), P(None, "col"))
    return jax.shard_map(on_device, mesh=mesh, in_specs=in_specs, out_specs=out_specs, check_vma=False)
```

```python
import functools

import jax
import jax.numpy as jnp
from jax import lax
from jax.experimental import pallas as pl
from jax.experimental.pallas import tpu as pltpu
from jax.sharding import PartitionSpec as P

BLK = 128
MESH = pl.DeviceIdType.MESH
F32 = jnp.float32
BF16 = jnp.bfloat16
KSTEP = 512


def split(x):
    hi = x.astype(BF16)
    return hi, (x - hi.astype(F32)).astype(BF16)


def dot3(left, right, dims):
    lh, ll = split(left)
    rh, rl = split(right)
    g = functools.partial(lax.dot_general, dimension_numbers=(dims, ((), ())), preferred_element_type=F32)
    return g(lh, rh) + (g(lh, rl) + g(ll, rh))


class Sends:
    def __init__(self, sems):
        self.sems = sems
        self.started = []

    def __call__(self, src, dst, recv, device):
        copy = pltpu.make_async_remote_copy(
            src_ref=src, dst_ref=dst, send_sem=self.sems.at[len(self.started)], recv_sem=recv,
            device_id=device, device_id_type=MESH,
        )
        copy.start()
        self.started.append(copy)
        return copy

    def finish(self):
        for copy in self.started:
            copy.wait_send()


def update_kernel(
    k_hbm, one_hbm, two_hbm, coupling, diag_one, diag_two, present_one, present_two,
    x1_out, x2_out, first_out, cross_out, second_out,
    k_f32, k_hi, k_lo, panels, mask, y, y_first, y_second, half_out, half_in, own, turned, y_two,
    pieces, mate_pieces, blocks, mate_blocks, slices, c_split, sums, s_first, s_second, rest, r_first, r_second,
    z_pair, z_in, over_g, g_in, gathered,
    local_sem, send_sem, recv_sem, x_sem, z_sem, p_send, p_recv, mate_sem, sum_sem, rest_sem, tail_sem, end_sem,
):
    row = lax.axis_index("row")
    col = lax.axis_index("col")
    g0, y0, k0 = row // 8, (row // 2) % 4, row % 2
    z0, x0 = col // 4, col % 4

    def at(g, yy, k):
        return ((g % 4) * 8 + (yy % 4) * 2 + k, col)

    y_up, y_down = at(g0, y0 + 1, k0), at(g0, y0 + 3, k0)
    g_up, g_down = at(g0 + 1, y0, k0), at(g0 + 3, y0, k0)
    sibling = at(g0, y0, 1 - k0)
    x_up, x_down = (row, z0 * 4 + (x0 + 1) % 4), (row, z0 * 4 + (x0 + 3) % 4)
    y_far, g_far = at(g0, y0 + 2, k0), at(g0 + 2, y0, k0)
    z_mate = (row, (1 - z0) * 4 + x0)
    p_target = (col * 4 + row // 8, row % 8)
    p_source = ((row % 4) * 8 + col, row // 4)
    stays = jnp.logical_and(p_target[0] == row, p_target[1] == col)

    k_copy = pltpu.make_async_copy(k_hbm, k_f32, local_sem.at[0])
    k_copy.start()
    firsts = [
        pltpu.make_async_copy(one_hbm, panels.at[g0, 0, y0, k0], local_sem.at[1]),
        pltpu.make_async_copy(two_hbm, panels.at[g0, 1, y0, k0], local_sem.at[2]),
    ]
    for copy in firsts:
        copy.start()

    barrier = pltpu.get_barrier_semaphore()
    for device in (y_up, y_down, y_far, g_up, g_down, g_far, sibling, x_up, x_down, z_mate):
        pl.semaphore_signal(barrier, inc=1, device_id=device, device_id_type=MESH)

    @pl.when(jnp.logical_not(stays))
    def _():
        pl.semaphore_signal(barrier, inc=1, device_id=p_target, device_id_type=MESH)
        pl.semaphore_signal(barrier, inc=1, device_id=p_source, device_id_type=MESH)

    pl.semaphore_wait(barrier, jnp.where(stays, 10, 12))
    for copy in firsts:
        copy.wait()

    send = Sends(send_sem)

    def landed(ref, sem):
        pltpu.make_async_remote_copy(
            src_ref=ref, dst_ref=ref, send_sem=send_sem.at[0], recv_sem=sem, device_id=sibling, device_id_type=MESH
        ).wait_recv()

    def ring_start(src, me, up, down, first, second, sem):
        send(src((me + 2) % 4, 0), first.at[0], sem.at[0], up)
        send(src((me + 2) % 4, 1), first.at[1], sem.at[1], down)
        send(src((me + 1) % 4, 1), second.at[0, 1], sem.at[3], up)
        send(src((me + 3) % 4, 0), second.at[1, 0], sem.at[4], down)

    def ring_middle(src, me, up, down, first, second, sem):
        landed(first.at[0], sem.at[0])
        src((me + 1) % 4, 0)[...] += first[0]
        send(src((me + 1) % 4, 0), second.at[0, 0], sem.at[2], up)
        landed(first.at[1], sem.at[1])
        src((me + 3) % 4, 1)[...] += first[1]
        send(src((me + 3) % 4, 1), second.at[1, 1], sem.at[5], down)

    def ring_wait(second, sem):
        for a in (0, 1):
            for b in (0, 1):
                landed(second.at[a, b], sem.at[2 + 2 * a + b])

    def part(g, p, yy, k):
        return panels.at[g % 4, p, yy % 4, k]

    def push(g, p, yy, k, device):
        ref = part(g, p, yy, k)
        send(ref, ref, recv_sem.at[g % 4, p, yy % 4, k], device)

    def arrive(g, p, yy, k):
        ref = part(g, p, yy, k)
        landed(ref, recv_sem.at[g % 4, p, yy % 4, k])

    def spread_y(g):
        for p in (0, 1):
            push(g, p, y0, k0, y_up)
            push(g, 1 - p, y0, k0, y_down)
        push(g, 0, y0, k0, sibling)
        push(g, 1, y0, k0, sibling)

    def relay_y(g):
        arrive(g, 0, y0 + 3, k0)
        push(g, 0, y0 + 3, k0, y_up)
        push(g, 0, y0 + 3, k0, sibling)
        arrive(g, 1, y0 + 1, k0)
        push(g, 1, y0 + 1, k0, y_down)
        push(g, 1, y0 + 1, k0, sibling)
        arrive(g, 1, y0 + 3, k0)
        push(g, 1, y0 + 3, k0, sibling)
        arrive(g, 0, y0 + 1, k0)
        push(g, 0, y0 + 1, k0, sibling)

    def end_y(g):
        for p in (0, 1):
            arrive(g, p, y0 + 2, k0)
            push(g, p, y0 + 2, k0, sibling)

    def x_ring(t):
        return (lambda x, z: y.at[t, z, x]), x0, x_up, x_down, y_first.at[t], y_second.at[t], x_sem.at[t]

    def compute(t, g):
        for yy in range(4):
            for p in (0, 1):
                arrive(g, p, y0 + yy, 1 - k0)
        group = g % 4
        y_ref = y.at[t]

        def step(i, carry):
            lanes = pl.ds(pl.multiple_of(i * KSTEP, KSTEP), KSTEP)
            block = panels[group, :, :, :, :, lanes].reshape(2, 16, 8, KSTEP)
            block = (block * mask[:, :, lanes][:, None]).reshape(256, KSTEP)
            ph, plo = split(block)
            kh, kl = k_hi[:, lanes], k_lo[:, lanes]
            dims = (((1,), (1,)), ((), ()))
            g2 = functools.partial(lax.dot_general, dimension_numbers=dims, preferred_element_type=F32)
            total = (g2(kh, ph) + g2(kl, ph) + g2(kh, plo)).reshape(2, 4, 80, 256)

            @pl.when(i == 0)
            def _():
                y_ref[...] = total

            @pl.when(i > 0)
            def _():
                y_ref[...] += total

            return carry

        lax.fori_loop(0, 2560 // KSTEP, step, 0)
        ring_start(*x_ring(t))
        start = jnp.minimum((row * 80) // BLK, 2560 // BLK - 2) * BLK
        lanes = pl.ds(pl.multiple_of(start, BLK), 256)
        window = panels[group, :, :, :, :, lanes].reshape(2, 16, 8, 256)
        window = (window * mask[:, :, lanes][:, None]).reshape(256, 256)
        turned[t] = window.T
        piece = turned.at[t, pl.ds(pl.multiple_of(row * 80 - start, 8), 80)]

        @pl.when(stays)
        def _():
            copy = pltpu.make_async_copy(piece, pieces.at[group], local_sem.at[3])
            copy.start()
            copy.wait()

        @pl.when(jnp.logical_not(stays))
        def _():
            pltpu.make_async_remote_copy(
                src_ref=piece, dst_ref=pieces.at[group], send_sem=p_send.at[t], recv_sem=p_recv.at[group],
                device_id=p_target, device_id_type=MESH,
            ).start()

    def reduce_x(t):
        ring_wait(y_second.at[t], x_sem.at[t])

        def total(z):
            return y[t, z, x0] + y_second[t, 0, z] + y_second[t, 1, z]

        half_out[t] = total(1 - z0)
        send(half_out.at[t], half_in.at[t], z_sem.at[t], z_mate)
        own[t] = total(z0)

    def finish_y(t, g):
        landed(half_in.at[t], z_sem.at[t])
        done = own[t] + half_in[t]
        lanes = pl.ds(pl.multiple_of((g % 4) * BLK, BLK), BLK)
        blocks[0, :, lanes] = -done[:, :BLK]
        y_two[:, lanes] = done[:, BLK:]

    order = (g0, g0 + 1, g0 + 3, g0 + 2)

    for p in (0, 1):
        push(g0, p, y0, k0, y_up)
        push(g0, 1 - p, y0, k0, y_down)
        push(g0, p, y0, k0, g_up)
        push(g0, 1 - p, y0, k0, g_down)
        push(g0, p, y0, k0, sibling)

    for p, present in ((0, present_one), (1, present_two)):
        for j in range(2560 // BLK):
            value = present[col * (2560 // BLK) + j].astype(F32)
            mask[p, :, j * BLK:(j + 1) * BLK] = jnp.full((8, BLK), value, F32)
    k_copy.wait()

    def split_rows(i, carry):
        rows = pl.ds(pl.multiple_of(i * 32, 32), 32)
        hi, lo = split(k_f32[rows, :])
        k_hi[rows, :] = hi
        k_lo[rows, :] = lo
        return carry

    lax.fori_loop(0, 20, split_rows, 0)
    hi, lo = split(coupling[...])
    c_split[0] = hi
    c_split[1] = lo
    pair = pl.ds(pl.multiple_of((col // 2) * BLK, BLK), BLK)
    for i, ref in enumerate((coupling, diag_one, diag_two)):
        slices[i] = ref[:, pair].T
    mine = pl.ds(pl.multiple_of((col % 2) * 64, 64), 64)

    relay_y(order[0])
    arrive(g0 + 3, 0, y0, k0)
    push(g0 + 3, 0, y0, k0, g_up)
    arrive(g0 + 1, 1, y0, k0)
    push(g0 + 1, 1, y0, k0, g_down)
    end_y(order[0])
    arrive(g0 + 1, 0, y0, k0)
    spread_y(order[1])
    compute(0, order[0])
    relay_y(order[1])
    arrive(g0 + 3, 1, y0, k0)
    spread_y(order[2])
    ring_middle(*x_ring(0))
    end_y(order[1])
    compute(1, order[1])
    reduce_x(0)
    relay_y(order[2])
    arrive(g0 + 2, 0, y0, k0)
    arrive(g0 + 2, 1, y0, k0)
    spread_y(order[3])
    ring_middle(*x_ring(1))
    end_y(order[2])
    compute(2, order[2])
    reduce_x(1)
    finish_y(0, order[0])
    relay_y(order[3])
    ring_middle(*x_ring(2))
    diag_coupled = dot3(slices[0, mine, :], diag_one[...], ((1,), (1,)))
    end_y(order[3])
    compute(3, order[3])
    reduce_x(2)
    finish_y(1, order[1])
    ring_middle(*x_ring(3))
    finish_y(2, order[2])
    reduce_x(3)
    finish_y(3, order[3])

    def times_coupling(left):
        lh, ll = split(left)
        g = functools.partial(jnp.dot, preferred_element_type=F32)
        return g(lh, c_split[0]) + (g(lh, c_split[1]) + g(ll, c_split[0]))

    blocks[1] = -(y_two[...] + times_coupling(blocks[0]))
    send(blocks, mate_blocks, mate_sem.at[0], sibling)

    @pl.when(jnp.logical_not(stays))
    def _():
        for t in range(4):
            copy = pltpu.make_async_remote_copy(
                src_ref=turned.at[t, pl.ds(0, 80)], dst_ref=pieces.at[t], send_sem=p_send.at[t],
                recv_sem=p_recv.at[t], device_id=p_target, device_id_type=MESH,
            )
            copy.wait_send()
            copy.wait_recv()

    send(pieces.at[pl.ds(2 * (1 - k0), 2)], mate_pieces, mate_sem.at[1], sibling)
    x1_out[...] = blocks[0]
    x2_out[...] = blocks[1]
    landed(mate_pieces, mate_sem.at[1])
    landed(mate_blocks, mate_sem.at[0])

    for side in (0, 1):
        lanes = slice(side * BLK, side * BLK + BLK)
        right = jnp.concatenate(
            [
                jnp.concatenate([pieces[2 * k0], pieces[2 * k0 + 1]], axis=1),
                jnp.concatenate([mate_pieces[0], mate_pieces[1]], axis=1),
            ],
            axis=0,
        )
        if side == 0:
            one = jnp.concatenate([right[:, 0:128], right[:, 256:384]], axis=1)
            two = jnp.concatenate([right[:, 128:256], right[:, 384:512]], axis=1)
            left = [jnp.concatenate([blocks[i], mate_blocks[i]], axis=0) for i in (0, 1)]
            products = [
                dot3(left[i], p, ((0,), (0,))).reshape(2, 4, 4, 16, 256) for i, p in ((0, one), (1, one), (1, two))
            ]
        for j, value in enumerate(products):
            for z in (0, 1):
                for w in range(4):
                    if side == 0:
                        sums[0, w, z, :, j] = value[z, w, :, :, :BLK]
                    else:
                        sums[1, w, z, :, j] = value[z, :, w, :, BLK:]

    ring_x, ring_y = (x0, x_up, x_down), (y0, y_up, y_down)
    whole = [
        ((lambda w, z, side=side: sums.at[side, w, z]), *ring, s_first.at[side], s_second.at[side], sum_sem.at[side])
        for side, ring in ((0, ring_x), (1, ring_y))
    ]
    part_of = [
        ((lambda w, z, side=side: rest.at[side, w, z]), *ring, r_first.at[side], r_second.at[side], rest_sem.at[side])
        for side, ring in ((0, ring_y), (1, ring_x))
    ]
    for side in (0, 1):
        ring_start(*whole[side])
    for side in (0, 1):
        ring_middle(*whole[side])
    for side in (0, 1):
        ring_wait(s_second.at[side], sum_sem.at[side])
        me = (x0, y0)[side]
        for z in (0, 1):
            rest[side, :, z] = sums[side, me, z] + s_second[side, 0, z] + s_second[side, 1, z]
        ring_start(*part_of[side])
    for side in (0, 1):
        ring_middle(*part_of[side])
    for side in (0, 1):
        ring_wait(r_second.at[side], rest_sem.at[side])
        me = (y0, x0)[side]
        for z in (0, 1):
            z_pair[z, side] = rest[side, me, z] + r_second[side, 0, z] + r_second[side, 1, z]
    send(z_pair.at[1 - z0], z_in, tail_sem.at[0], z_mate)
    landed(z_in, tail_sem.at[0])
    over_g[...] = z_pair[z0] + z_in[...]
    for d, device in enumerate((g_up, g_down, g_far)):
        send(over_g, g_in.at[d], tail_sem.at[1 + d], device)
    for d in range(3):
        landed(g_in.at[d], tail_sem.at[1 + d])
    even = over_g[...] + g_in[2]
    odd = g_in[0] + g_in[1]
    gathered[k0, y0] = even + odd
    mine_ref = gathered.at[k0, y0]
    for device in (y_up, y_down, y_far, sibling):
        send(mine_ref, mine_ref, end_sem.at[k0, y0], device)
    for d in (1, 3, 2):
        ref = gathered.at[k0, (y0 + d) % 4]
        landed(ref, end_sem.at[k0, (y0 + d) % 4])
        send(ref, ref, end_sem.at[k0, (y0 + d) % 4], sibling)
    for d in range(4):
        ref = gathered.at[1 - k0, (y0 + d) % 4]
        landed(ref, end_sem.at[1 - k0, (y0 + d) % 4])

    def total_of(j):
        return jnp.concatenate(
            [
                jnp.concatenate([gathered[k, w, side, j] for w in range(4)], axis=0)
                for k in (0, 1)
                for side in (0, 1)
            ],
            axis=1,
        )

    first_out[...] = slices[1, mine, :] - total_of(0)
    cross = -total_of(1) - diag_coupled
    cross_out[...] = cross
    second_out[...] = slices[2, mine, :] - total_of(2) - times_coupling(cross)
    send.finish()


def update(known_inverse, one, two, coupling, diag_one, diag_two, present_one, present_two):
    vmem = pl.BlockSpec(memory_space=pltpu.VMEM)
    hbm = pl.BlockSpec(memory_space=pl.ANY)
    smem = pl.BlockSpec(memory_space=pltpu.SMEM)
    dma = pltpu.SemaphoreType.DMA
    tall = jax.ShapeDtypeStruct((80, 512), F32)
    small = jax.ShapeDtypeStruct((64, 512), F32)
    return pl.pallas_call(
        update_kernel,
        out_shape=(tall, tall, small, small, small),
        in_specs=[hbm, hbm, hbm, vmem, vmem, vmem, smem, smem],
        out_specs=(vmem,) * 5,
        scratch_shapes=[
            pltpu.VMEM((640, 2560), F32),
            pltpu.VMEM((640, 2560), BF16),
            pltpu.VMEM((640, 2560), BF16),
            pltpu.VMEM((4, 2, 4, 2, 16, 2560), F32),
            pltpu.VMEM((2, 8, 2560), F32),
            pltpu.VMEM((4, 2, 4, 80, 256), F32),
            pltpu.VMEM((4, 2, 80, 256), F32),
            pltpu.VMEM((4, 2, 2, 80, 256), F32),
            pltpu.VMEM((4, 80, 256), F32),
            pltpu.VMEM((4, 80, 256), F32),
            pltpu.VMEM((4, 80, 256), F32),
            pltpu.VMEM((4, 256, 256), F32),
            pltpu.VMEM((80, 512), F32),
            pltpu.VMEM((4, 80, 256), F32),
            pltpu.VMEM((2, 80, 256), F32),
            pltpu.VMEM((2, 80, 512), F32),
            pltpu.VMEM((2, 80, 512), F32),
            pltpu.VMEM((3, 128, 512), F32),
            pltpu.VMEM((2, 512, 512), BF16),
            pltpu.VMEM((2, 4, 2, 4, 3, 16, 128), F32),
            pltpu.VMEM((2, 2, 4, 3, 16, 128), F32),
            pltpu.VMEM((2, 2, 2, 4, 3, 16, 128), F32),
            pltpu.VMEM((2, 4, 2, 3, 16, 128), F32),
            pltpu.VMEM((2, 2, 3, 16, 128), F32),
            pltpu.VMEM((2, 2, 2, 3, 16, 128), F32),
            pltpu.VMEM((2, 2, 3, 16, 128), F32),
            pltpu.VMEM((2, 3, 16, 128), F32),
            pltpu.VMEM((2, 3, 16, 128), F32),
            pltpu.VMEM((3, 2, 3, 16, 128), F32),
            pltpu.VMEM((2, 4, 2, 3, 16, 128), F32),
            dma((4,)),
            dma((140,)),
            dma((4, 2, 4, 2)),
            dma((4, 6)),
            dma((4,)),
            dma((4,)),
            dma((4,)),
            dma((2,)),
            dma((2, 6)),
            dma((2, 6)),
            dma((4,)),
            dma((2, 4)),
        ],
        compiler_params=pltpu.CompilerParams(
            collective_id=0, has_side_effects=True, vmem_limit_bytes=56 * 2**20
        ),
        name="update",
    )(known_inverse, one, two, coupling, diag_one, diag_two, present_one, present_two)


def on_device(known_inverse, first_panel, second_panel, coupling, first_diag, second_diag, first_present, second_present):
    x1, x2, first, cross, second = update(
        known_inverse, first_panel.T, second_panel.T, coupling, first_diag, second_diag, first_present, second_present
    )
    return x1, first.T, x2, cross.T, second.T


def solution(mesh):
    in_specs = (P("row", "col"), P("col", "row"), P("col", "row"), P(), P(), P(), P(), P())
    out_specs = (P(("row", "col"), None), P(None, "col"), P(("row", "col"), None), P(None, "col"), P(None, "col"))
    return jax.shard_map(on_device, mesh=mesh, in_specs=in_specs, out_specs=out_specs, check_vma=False)
```

```python
import functools

import jax
import jax.numpy as jnp
from jax import lax
from jax.experimental import pallas as pl
from jax.experimental.pallas import tpu as pltpu
from jax.sharding import PartitionSpec as P

BLK = 128
MESH = pl.DeviceIdType.MESH
F32 = jnp.float32
BF16 = jnp.bfloat16
KSTEP = 512


def split(x):
    hi = x.astype(BF16)
    return hi, (x - hi.astype(F32)).astype(BF16)


def dot3(left, right, dims):
    lh, ll = split(left)
    rh, rl = split(right)
    g = functools.partial(lax.dot_general, dimension_numbers=(dims, ((), ())), preferred_element_type=F32)
    return g(lh, rh) + (g(lh, rl) + g(ll, rh))


class Sends:
    def __init__(self, sems):
        self.sems = sems
        self.started = []

    def __call__(self, src, dst, recv, device):
        copy = pltpu.make_async_remote_copy(
            src_ref=src, dst_ref=dst, send_sem=self.sems.at[len(self.started)], recv_sem=recv,
            device_id=device, device_id_type=MESH,
        )
        copy.start()
        self.started.append(copy)
        return copy

    def finish(self):
        for copy in self.started:
            copy.wait_send()


def update_kernel(
    k_hbm, one_hbm, two_hbm, coupling, diag_one, diag_two, present_one, present_two,
    x1_out, x2_out, first_out, cross_out, second_out,
    k_f32, k_hi, k_lo, panels, mask, y, y_first, y_second, half_out, half_in, own, turned, y_two,
    pieces, mate_pieces, blocks, mate_blocks, slices, c_split, sums, s_first, s_second, rest, r_first, r_second,
    z_pair, z_in, over_g, g_in, gathered,
    local_sem, send_sem, recv_sem, x_sem, z_sem, p_send, p_recv, mate_sem, sum_sem, rest_sem, tail_sem, end_sem,
):
    row = lax.axis_index("row")
    col = lax.axis_index("col")
    g0, y0, k0 = row // 8, (row // 2) % 4, row % 2
    z0, x0 = col // 4, col % 4

    def at(g, yy, k):
        return ((g % 4) * 8 + (yy % 4) * 2 + k, col)

    y_up, y_down = at(g0, y0 + 1, k0), at(g0, y0 + 3, k0)
    g_up, g_down = at(g0 + 1, y0, k0), at(g0 + 3, y0, k0)
    sibling = at(g0, y0, 1 - k0)
    x_up, x_down = (row, z0 * 4 + (x0 + 1) % 4), (row, z0 * 4 + (x0 + 3) % 4)
    y_far, g_far = at(g0, y0 + 2, k0), at(g0 + 2, y0, k0)
    z_mate = (row, (1 - z0) * 4 + x0)
    hands_out = g0 == col // 2
    level = (y0 // 2) == (col % 2)
    y_to = jnp.where(level, y0, 3 - y0)
    to_row = g0 * 8 + y_to * 2 + k0
    x_first = x0 + jnp.where(level, 0, 2)

    def to_col(i):
        return (i // 2) * 4 + (x_first + i % 2) % 4

    giver_col = row // 4
    y_from = jnp.where((x0 - giver_col % 4 + 4) % 4 < 2, y0, 3 - y0)
    giver = (g0 * 8 + y_from * 2 + k0, giver_col)
    stays = jnp.logical_and(giver[0] == row, giver_col == col)

    k_copy = pltpu.make_async_copy(k_hbm, k_f32, local_sem.at[0])
    k_copy.start()
    firsts = [
        pltpu.make_async_copy(one_hbm, panels.at[g0, 0, y0, k0], local_sem.at[1]),
        pltpu.make_async_copy(two_hbm, panels.at[g0, 1, y0, k0], local_sem.at[2]),
    ]
    for copy in firsts:
        copy.start()

    barrier = pltpu.get_barrier_semaphore()
    for device in (y_up, y_down, y_far, g_up, g_down, g_far, sibling, x_up, x_down, z_mate):
        pl.semaphore_signal(barrier, inc=1, device_id=device, device_id_type=MESH)

    @pl.when(hands_out)
    def _():
        for i in range(4):
            @pl.when(jnp.logical_not(jnp.logical_and(to_row == row, to_col(i) == col)))
            def _():
                pl.semaphore_signal(barrier, inc=1, device_id=(to_row, to_col(i)), device_id_type=MESH)

    @pl.when(jnp.logical_not(stays))
    def _():
        pl.semaphore_signal(barrier, inc=1, device_id=giver, device_id_type=MESH)

    extra = jnp.where(hands_out, 4, 0) + jnp.where(stays, -1, 1)
    pl.semaphore_wait(barrier, 10 + extra)
    for copy in firsts:
        copy.wait()

    send = Sends(send_sem)

    def landed(ref, sem):
        pltpu.make_async_remote_copy(
            src_ref=ref, dst_ref=ref, send_sem=send_sem.at[0], recv_sem=sem, device_id=sibling, device_id_type=MESH
        ).wait_recv()

    def ring_start(src, me, up, down, first, second, sem):
        send(src((me + 2) % 4, 0), first.at[0], sem.at[0], up)
        send(src((me + 2) % 4, 1), first.at[1], sem.at[1], down)
        send(src((me + 1) % 4, 1), second.at[0, 1], sem.at[3], up)
        send(src((me + 3) % 4, 0), second.at[1, 0], sem.at[4], down)

    def ring_middle(src, me, up, down, first, second, sem):
        landed(first.at[0], sem.at[0])
        src((me + 1) % 4, 0)[...] += first[0]
        send(src((me + 1) % 4, 0), second.at[0, 0], sem.at[2], up)
        landed(first.at[1], sem.at[1])
        src((me + 3) % 4, 1)[...] += first[1]
        send(src((me + 3) % 4, 1), second.at[1, 1], sem.at[5], down)

    def ring_wait(second, sem):
        for a in (0, 1):
            for b in (0, 1):
                landed(second.at[a, b], sem.at[2 + 2 * a + b])

    def part(g, p, yy, k):
        return panels.at[g % 4, p, yy % 4, k]

    def push(g, p, yy, k, device):
        ref = part(g, p, yy, k)
        send(ref, ref, recv_sem.at[g % 4, p, yy % 4, k], device)

    def arrive(g, p, yy, k):
        ref = part(g, p, yy, k)
        landed(ref, recv_sem.at[g % 4, p, yy % 4, k])

    def spread_y(g):
        for p in (0, 1):
            push(g, p, y0, k0, y_up)
            push(g, 1 - p, y0, k0, y_down)
        push(g, 0, y0, k0, sibling)
        push(g, 1, y0, k0, sibling)

    def relay_y(g):
        arrive(g, 0, y0 + 3, k0)
        push(g, 0, y0 + 3, k0, y_up)
        push(g, 0, y0 + 3, k0, sibling)
        arrive(g, 1, y0 + 1, k0)
        push(g, 1, y0 + 1, k0, y_down)
        push(g, 1, y0 + 1, k0, sibling)
        arrive(g, 1, y0 + 3, k0)
        push(g, 1, y0 + 3, k0, sibling)
        arrive(g, 0, y0 + 1, k0)
        push(g, 0, y0 + 1, k0, sibling)

    def end_y(g):
        for p in (0, 1):
            arrive(g, p, y0 + 2, k0)
            push(g, p, y0 + 2, k0, sibling)

    def x_ring(t):
        return (lambda x, z: y.at[t, z, x]), x0, x_up, x_down, y_first.at[t], y_second.at[t], x_sem.at[t]

    def compute(t, g):
        for yy in range(4):
            for p in (0, 1):
                arrive(g, p, y0 + yy, 1 - k0)
        group = g % 4
        y_ref = y.at[t]

        def step(i, carry):
            lanes = pl.ds(pl.multiple_of(i * KSTEP, KSTEP), KSTEP)
            block = panels[group, :, :, :, :, lanes].reshape(2, 16, 8, KSTEP)
            block = (block * mask[:, :, lanes][:, None]).reshape(256, KSTEP)
            ph, plo = split(block)
            kh, kl = k_hi[:, lanes], k_lo[:, lanes]
            dims = (((1,), (1,)), ((), ()))
            g2 = functools.partial(lax.dot_general, dimension_numbers=dims, preferred_element_type=F32)
            total = (g2(kh, ph) + g2(kl, ph) + g2(kh, plo)).reshape(2, 4, 80, 256)

            @pl.when(i == 0)
            def _():
                y_ref[...] = total

            @pl.when(i > 0)
            def _():
                y_ref[...] += total

            return carry

        lax.fori_loop(0, 2560 // KSTEP, step, 0)
        ring_start(*x_ring(t))
        def hand(i):
            target = to_col(i)
            first_row = (((y_to % 2) * 2 + k0) * 8 + target) * 80
            start = jnp.minimum(first_row // BLK, 2560 // BLK - 2) * BLK
            lanes = pl.ds(pl.multiple_of(start, BLK), 256)
            window = panels[group, :, :, :, :, lanes].reshape(2, 16, 8, 256)
            window = (window * mask[:, :, lanes][:, None]).reshape(256, 256)
            turned[t, i] = window.T
            piece = turned.at[t, i, pl.ds(pl.multiple_of(first_row - start, 8), 80)]
            same = jnp.logical_and(to_row == row, target == col)

            @pl.when(same)
            def _():
                copy = pltpu.make_async_copy(piece, pieces.at[group], local_sem.at[3])
                copy.start()
                copy.wait()

            @pl.when(jnp.logical_not(same))
            def _():
                pltpu.make_async_remote_copy(
                    src_ref=piece, dst_ref=pieces.at[group], send_sem=p_send.at[t, i], recv_sem=p_recv.at[group],
                    device_id=(to_row, target), device_id_type=MESH,
                ).start()

        @pl.when(hands_out)
        def _():
            for i in range(4):
                hand(i)

    def reduce_x(t):
        ring_wait(y_second.at[t], x_sem.at[t])

        def total(z):
            return y[t, z, x0] + y_second[t, 0, z] + y_second[t, 1, z]

        half_out[t] = total(1 - z0)
        send(half_out.at[t], half_in.at[t], z_sem.at[t], z_mate)
        own[t] = total(z0)

    def finish_y(t, g):
        landed(half_in.at[t], z_sem.at[t])
        done = own[t] + half_in[t]
        lanes = pl.ds(pl.multiple_of((g % 4) * BLK, BLK), BLK)
        blocks[0, :, lanes] = -done[:, :BLK]
        y_two[:, lanes] = done[:, BLK:]

    order = (g0, g0 + 1, g0 + 3, g0 + 2)

    for p in (0, 1):
        push(g0, p, y0, k0, y_up)
        push(g0, 1 - p, y0, k0, y_down)
        push(g0, p, y0, k0, g_up)
        push(g0, 1 - p, y0, k0, g_down)
        push(g0, p, y0, k0, sibling)

    for p, present in ((0, present_one), (1, present_two)):
        for j in range(2560 // BLK):
            value = present[col * (2560 // BLK) + j].astype(F32)
            mask[p, :, j * BLK:(j + 1) * BLK] = jnp.full((8, BLK), value, F32)
    k_copy.wait()

    def split_rows(i, carry):
        rows = pl.ds(pl.multiple_of(i * 32, 32), 32)
        hi, lo = split(k_f32[rows, :])
        k_hi[rows, :] = hi
        k_lo[rows, :] = lo
        return carry

    lax.fori_loop(0, 20, split_rows, 0)
    hi, lo = split(coupling[...])
    c_split[0] = hi
    c_split[1] = lo
    pair = pl.ds(pl.multiple_of((col // 2) * BLK, BLK), BLK)
    for i, ref in enumerate((coupling, diag_one, diag_two)):
        slices[i] = ref[:, pair].T
    mine = pl.ds(pl.multiple_of((col % 2) * 64, 64), 64)

    relay_y(order[0])
    arrive(g0 + 3, 0, y0, k0)
    push(g0 + 3, 0, y0, k0, g_up)
    arrive(g0 + 1, 1, y0, k0)
    push(g0 + 1, 1, y0, k0, g_down)
    end_y(order[0])
    arrive(g0 + 1, 0, y0, k0)
    spread_y(order[1])
    compute(0, order[0])
    relay_y(order[1])
    arrive(g0 + 3, 1, y0, k0)
    spread_y(order[2])
    ring_middle(*x_ring(0))
    end_y(order[1])
    compute(1, order[1])
    reduce_x(0)
    relay_y(order[2])
    arrive(g0 + 2, 0, y0, k0)
    arrive(g0 + 2, 1, y0, k0)
    spread_y(order[3])
    ring_middle(*x_ring(1))
    end_y(order[2])
    compute(2, order[2])
    reduce_x(1)
    finish_y(0, order[0])
    relay_y(order[3])
    ring_middle(*x_ring(2))
    diag_coupled = dot3(slices[0, mine, :], diag_one[...], ((1,), (1,)))
    end_y(order[3])
    compute(3, order[3])
    reduce_x(2)
    finish_y(1, order[1])
    ring_middle(*x_ring(3))
    finish_y(2, order[2])
    reduce_x(3)
    finish_y(3, order[3])

    def times_coupling(left):
        lh, ll = split(left)
        g = functools.partial(jnp.dot, preferred_element_type=F32)
        return g(lh, c_split[0]) + (g(lh, c_split[1]) + g(ll, c_split[0]))

    blocks[1] = -(y_two[...] + times_coupling(blocks[0]))
    send(blocks, mate_blocks, mate_sem.at[0], sibling)

    @pl.when(jnp.logical_not(stays))
    def _():
        for g in range(4):
            landed(pieces.at[g], p_recv.at[g])

    send(pieces.at[pl.ds(2 * (1 - k0), 2)], mate_pieces, mate_sem.at[1], sibling)
    x1_out[...] = blocks[0]
    x2_out[...] = blocks[1]
    landed(mate_pieces, mate_sem.at[1])
    landed(mate_blocks, mate_sem.at[0])

    for side in (0, 1):
        lanes = slice(side * BLK, side * BLK + BLK)
        right = jnp.concatenate(
            [
                jnp.concatenate([pieces[2 * k0], pieces[2 * k0 + 1]], axis=1),
                jnp.concatenate([mate_pieces[0], mate_pieces[1]], axis=1),
            ],
            axis=0,
        )
        if side == 0:
            one = jnp.concatenate([right[:, 0:128], right[:, 256:384]], axis=1)
            two = jnp.concatenate([right[:, 128:256], right[:, 384:512]], axis=1)
            left = [jnp.concatenate([blocks[i], mate_blocks[i]], axis=0) for i in (0, 1)]
            products = [
                dot3(left[i], p, ((0,), (0,))).reshape(2, 4, 4, 16, 256) for i, p in ((0, one), (1, one), (1, two))
            ]
        for j, value in enumerate(products):
            for z in (0, 1):
                for w in range(4):
                    if side == 0:
                        sums[0, w, z, :, j] = value[z, w, :, :, :BLK]
                    else:
                        sums[1, w, z, :, j] = value[z, :, w, :, BLK:]

    ring_x, ring_y = (x0, x_up, x_down), (y0, y_up, y_down)
    whole = [
        ((lambda w, z, side=side: sums.at[side, w, z]), *ring, s_first.at[side], s_second.at[side], sum_sem.at[side])
        for side, ring in ((0, ring_x), (1, ring_y))
    ]
    part_of = [
        ((lambda w, z, side=side: rest.at[side, w, z]), *ring, r_first.at[side], r_second.at[side], rest_sem.at[side])
        for side, ring in ((0, ring_y), (1, ring_x))
    ]
    for side in (0, 1):
        ring_start(*whole[side])
    for side in (0, 1):
        ring_middle(*whole[side])
    for side in (0, 1):
        ring_wait(s_second.at[side], sum_sem.at[side])
        me = (x0, y0)[side]
        for z in (0, 1):
            rest[side, :, z] = sums[side, me, z] + s_second[side, 0, z] + s_second[side, 1, z]
        ring_start(*part_of[side])
    for side in (0, 1):
        ring_middle(*part_of[side])
    for side in (0, 1):
        ring_wait(r_second.at[side], rest_sem.at[side])
        me = (y0, x0)[side]
        for z in (0, 1):
            z_pair[z, side] = rest[side, me, z] + r_second[side, 0, z] + r_second[side, 1, z]
    send(z_pair.at[1 - z0], z_in, tail_sem.at[0], z_mate)
    landed(z_in, tail_sem.at[0])
    over_g[...] = z_pair[z0] + z_in[...]
    for d, device in enumerate((g_up, g_down, g_far)):
        send(over_g, g_in.at[d], tail_sem.at[1 + d], device)
    for d in range(3):
        landed(g_in.at[d], tail_sem.at[1 + d])
    even = over_g[...] + g_in[2]
    odd = g_in[0] + g_in[1]
    gathered[k0, y0] = even + odd
    mine_ref = gathered.at[k0, y0]
    for device in (y_up, y_down, y_far, sibling):
        send(mine_ref, mine_ref, end_sem.at[k0, y0], device)
    for d in (1, 3, 2):
        ref = gathered.at[k0, (y0 + d) % 4]
        landed(ref, end_sem.at[k0, (y0 + d) % 4])
        send(ref, ref, end_sem.at[k0, (y0 + d) % 4], sibling)
    for d in range(4):
        ref = gathered.at[1 - k0, (y0 + d) % 4]
        landed(ref, end_sem.at[1 - k0, (y0 + d) % 4])

    def total_of(j):
        return jnp.concatenate(
            [
                jnp.concatenate([gathered[k, w, side, j] for w in range(4)], axis=0)
                for k in (0, 1)
                for side in (0, 1)
            ],
            axis=1,
        )

    first_out[...] = slices[1, mine, :] - total_of(0)
    cross = -total_of(1) - diag_coupled
    cross_out[...] = cross
    second_out[...] = slices[2, mine, :] - total_of(2) - times_coupling(cross)
    send.finish()

    @pl.when(hands_out)
    def _():
        for i in range(4):
            @pl.when(jnp.logical_not(jnp.logical_and(to_row == row, to_col(i) == col)))
            def _():
                for t in range(4):
                    pltpu.make_async_remote_copy(
                        src_ref=turned.at[t, i, pl.ds(0, 80)], dst_ref=pieces.at[t], send_sem=p_send.at[t, i],
                        recv_sem=p_recv.at[t], device_id=giver, device_id_type=MESH,
                    ).wait_send()


def update(known_inverse, one, two, coupling, diag_one, diag_two, present_one, present_two):
    vmem = pl.BlockSpec(memory_space=pltpu.VMEM)
    hbm = pl.BlockSpec(memory_space=pl.ANY)
    smem = pl.BlockSpec(memory_space=pltpu.SMEM)
    dma = pltpu.SemaphoreType.DMA
    tall = jax.ShapeDtypeStruct((80, 512), F32)
    small = jax.ShapeDtypeStruct((64, 512), F32)
    return pl.pallas_call(
        update_kernel,
        out_shape=(tall, tall, small, small, small),
        in_specs=[hbm, hbm, hbm, vmem, vmem, vmem, smem, smem],
        out_specs=(vmem,) * 5,
        scratch_shapes=[
            pltpu.VMEM((640, 2560), F32),
            pltpu.VMEM((640, 2560), BF16),
            pltpu.VMEM((640, 2560), BF16),
            pltpu.VMEM((4, 2, 4, 2, 16, 2560), F32),
            pltpu.VMEM((2, 8, 2560), F32),
            pltpu.VMEM((4, 2, 4, 80, 256), F32),
            pltpu.VMEM((4, 2, 80, 256), F32),
            pltpu.VMEM((4, 2, 2, 80, 256), F32),
            pltpu.VMEM((4, 80, 256), F32),
            pltpu.VMEM((4, 80, 256), F32),
            pltpu.VMEM((4, 80, 256), F32),
            pltpu.VMEM((4, 4, 256, 256), F32),
            pltpu.VMEM((80, 512), F32),
            pltpu.VMEM((4, 80, 256), F32),
            pltpu.VMEM((2, 80, 256), F32),
            pltpu.VMEM((2, 80, 512), F32),
            pltpu.VMEM((2, 80, 512), F32),
            pltpu.VMEM((3, 128, 512), F32),
            pltpu.VMEM((2, 512, 512), BF16),
            pltpu.VMEM((2, 4, 2, 4, 3, 16, 128), F32),
            pltpu.VMEM((2, 2, 4, 3, 16, 128), F32),
            pltpu.VMEM((2, 2, 2, 4, 3, 16, 128), F32),
            pltpu.VMEM((2, 4, 2, 3, 16, 128), F32),
            pltpu.VMEM((2, 2, 3, 16, 128), F32),
            pltpu.VMEM((2, 2, 2, 3, 16, 128), F32),
            pltpu.VMEM((2, 2, 3, 16, 128), F32),
            pltpu.VMEM((2, 3, 16, 128), F32),
            pltpu.VMEM((2, 3, 16, 128), F32),
            pltpu.VMEM((3, 2, 3, 16, 128), F32),
            pltpu.VMEM((2, 4, 2, 3, 16, 128), F32),
            dma((4,)),
            dma((140,)),
            dma((4, 2, 4, 2)),
            dma((4, 6)),
            dma((4,)),
            dma((4, 4)),
            dma((4,)),
            dma((2,)),
            dma((2, 6)),
            dma((2, 6)),
            dma((4,)),
            dma((2, 4)),
        ],
        compiler_params=pltpu.CompilerParams(
            collective_id=0, has_side_effects=True, vmem_limit_bytes=56 * 2**20
        ),
        name="update",
    )(known_inverse, one, two, coupling, diag_one, diag_two, present_one, present_two)


def emit_kernel(*refs):
    for source, target in zip(refs[:5], refs[5:]):
        target[...] = source[...]


def emit(*arrays):
    vmem = pl.BlockSpec(memory_space=pltpu.VMEM)
    return pl.pallas_call(
        emit_kernel,
        out_shape=tuple(jax.ShapeDtypeStruct(a.shape, a.dtype) for a in arrays),
        in_specs=[vmem] * 5,
        out_specs=(vmem,) * 5,
        name="emit",
    )(*arrays)


def on_device(known_inverse, first_panel, second_panel, coupling, first_diag, second_diag, first_present, second_present):
    x1, x2, first, cross, second = emit(
        *update(
            known_inverse, first_panel.T, second_panel.T, coupling, first_diag, second_diag, first_present, second_present
        )
    )
    return x1, first.T, x2, cross.T, second.T


def solution(mesh):
    in_specs = (P("row", "col"), P("col", "row"), P("col", "row"), P(), P(), P(), P(), P())
    out_specs = (P(("row", "col"), None), P(None, "col"), P(("row", "col"), None), P(None, "col"), P(None, "col"))
    return jax.shard_map(on_device, mesh=mesh, in_specs=in_specs, out_specs=out_specs, check_vma=False)
```

```python
import functools

import jax
import jax.numpy as jnp
from jax import lax
from jax.experimental import pallas as pl
from jax.experimental.pallas import tpu as pltpu
from jax.sharding import PartitionSpec as P

BLK = 128
MESH = pl.DeviceIdType.MESH
F32 = jnp.float32
BF16 = jnp.bfloat16
KSTEP = 512


def split(x):
    hi = x.astype(BF16)
    return hi, (x - hi.astype(F32)).astype(BF16)


def dot3(left, right, dims):
    lh, ll = split(left)
    rh, rl = split(right)
    g = functools.partial(lax.dot_general, dimension_numbers=(dims, ((), ())), preferred_element_type=F32)
    return g(lh, rh) + (g(lh, rl) + g(ll, rh))


class Sends:
    def __init__(self, sems):
        self.sems = sems
        self.started = []

    def __call__(self, src, dst, recv, device):
        copy = pltpu.make_async_remote_copy(
            src_ref=src, dst_ref=dst, send_sem=self.sems.at[len(self.started)], recv_sem=recv,
            device_id=device, device_id_type=MESH,
        )
        copy.start()
        self.started.append(copy)
        return copy

    def finish(self):
        for copy in self.started:
            copy.wait_send()


def update_kernel(
    k_hbm, one_hbm, two_hbm, c_hbm, d_one_hbm, d_two_hbm, present_one, present_two,
    x1_out, x2_out, first_out, cross_out, second_out,
    coupling, diag_one, diag_two,
    k_f32, k_hi, k_lo, panels, mask, y, y_first, y_second, half_out, half_in, own, turned, y_two,
    pieces, mate_pieces, blocks, mate_blocks, slices, c_split, sums_a, a_first, a_second, sums_b, b_first, b_second, rest, r_first, r_second,
    z_pair, z_in, over_g, g_in, gathered,
    local_sem, send_sem, recv_sem, x_sem, z_sem, p_send, p_recv, mate_sem, sum_sem, rest_sem, tail_sem, end_sem,
):
    row = lax.axis_index("row")
    col = lax.axis_index("col")
    g0, y0, k0 = row // 8, (row // 2) % 4, row % 2
    z0, x0 = col // 4, col % 4

    def at(g, yy, k):
        return ((g % 4) * 8 + (yy % 4) * 2 + k, col)

    y_up, y_down = at(g0, y0 + 1, k0), at(g0, y0 + 3, k0)
    g_up, g_down = at(g0 + 1, y0, k0), at(g0 + 3, y0, k0)
    sibling = at(g0, y0, 1 - k0)
    x_up, x_down = (row, z0 * 4 + (x0 + 1) % 4), (row, z0 * 4 + (x0 + 3) % 4)
    y_far, g_far = at(g0, y0 + 2, k0), at(g0 + 2, y0, k0)
    z_mate = (row, (1 - z0) * 4 + x0)
    hands_out = g0 == col // 2
    level = (y0 // 2) == (col % 2)
    y_to = jnp.where(level, y0, 3 - y0)
    to_row = g0 * 8 + y_to * 2 + k0
    x_first = x0 + jnp.where(level, 0, 2)

    def to_col(i):
        return (i // 2) * 4 + (x_first + i % 2) % 4

    giver_col = row // 4
    y_from = jnp.where((x0 - giver_col % 4 + 4) % 4 < 2, y0, 3 - y0)
    giver = (g0 * 8 + y_from * 2 + k0, giver_col)
    stays = jnp.logical_and(giver[0] == row, giver_col == col)

    k_copy = pltpu.make_async_copy(k_hbm, k_f32, local_sem.at[0])
    firsts = [
        pltpu.make_async_copy(one_hbm, panels.at[g0, 0, y0, k0], local_sem.at[1]),
        pltpu.make_async_copy(two_hbm, panels.at[g0, 1, y0, k0], local_sem.at[2]),
    ]
    for copy in firsts:
        copy.start()

    barrier = pltpu.get_barrier_semaphore()
    for device in (y_up, y_down, y_far, g_up, g_down, g_far, sibling, x_up, x_down, z_mate):
        pl.semaphore_signal(barrier, inc=1, device_id=device, device_id_type=MESH)

    @pl.when(hands_out)
    def _():
        for i in range(4):
            @pl.when(jnp.logical_not(jnp.logical_and(to_row == row, to_col(i) == col)))
            def _():
                pl.semaphore_signal(barrier, inc=1, device_id=(to_row, to_col(i)), device_id_type=MESH)

    @pl.when(jnp.logical_not(stays))
    def _():
        pl.semaphore_signal(barrier, inc=1, device_id=giver, device_id_type=MESH)

    extra = jnp.where(hands_out, 4, 0) + jnp.where(stays, -1, 1)
    pl.semaphore_wait(barrier, 10 + extra)
    for copy in firsts:
        copy.wait()
    squares = [
        pltpu.make_async_copy(source, target, local_sem.at[i])
        for i, source, target in ((4, c_hbm, coupling), (5, d_one_hbm, diag_one), (6, d_two_hbm, diag_two))
    ]

    send = Sends(send_sem)

    def landed(ref, sem):
        pltpu.make_async_remote_copy(
            src_ref=ref, dst_ref=ref, send_sem=send_sem.at[0], recv_sem=sem, device_id=sibling, device_id_type=MESH
        ).wait_recv()

    def ring_start(src, me, up, down, first, second, sem):
        send(src((me + 2) % 4, 0), first.at[0], sem.at[0], up)
        send(src((me + 2) % 4, 1), first.at[1], sem.at[1], down)
        send(src((me + 1) % 4, 1), second.at[0, 1], sem.at[3], up)
        send(src((me + 3) % 4, 0), second.at[1, 0], sem.at[4], down)

    def ring_middle(src, me, up, down, first, second, sem):
        landed(first.at[0], sem.at[0])
        src((me + 1) % 4, 0)[...] += first[0]
        send(src((me + 1) % 4, 0), second.at[0, 0], sem.at[2], up)
        landed(first.at[1], sem.at[1])
        src((me + 3) % 4, 1)[...] += first[1]
        send(src((me + 3) % 4, 1), second.at[1, 1], sem.at[5], down)

    def ring_wait(second, sem):
        for a in (0, 1):
            for b in (0, 1):
                landed(second.at[a, b], sem.at[2 + 2 * a + b])

    def part(g, p, yy, k):
        return panels.at[g % 4, p, yy % 4, k]

    def push(g, p, yy, k, device):
        ref = part(g, p, yy, k)
        send(ref, ref, recv_sem.at[g % 4, p, yy % 4, k], device)

    def arrive(g, p, yy, k):
        ref = part(g, p, yy, k)
        landed(ref, recv_sem.at[g % 4, p, yy % 4, k])

    def spread_y(g):
        for p in (0, 1):
            push(g, p, y0, k0, y_up)
            push(g, 1 - p, y0, k0, y_down)
        push(g, 0, y0, k0, sibling)
        push(g, 1, y0, k0, sibling)

    def relay_y(g):
        arrive(g, 0, y0 + 3, k0)
        push(g, 0, y0 + 3, k0, y_up)
        push(g, 0, y0 + 3, k0, sibling)
        arrive(g, 1, y0 + 1, k0)
        push(g, 1, y0 + 1, k0, y_down)
        push(g, 1, y0 + 1, k0, sibling)
        arrive(g, 1, y0 + 3, k0)
        push(g, 1, y0 + 3, k0, sibling)
        arrive(g, 0, y0 + 1, k0)
        push(g, 0, y0 + 1, k0, sibling)

    def end_y(g):
        for p in (0, 1):
            arrive(g, p, y0 + 2, k0)
            push(g, p, y0 + 2, k0, sibling)

    def x_ring(t):
        return (lambda x, z: y.at[t, z, x]), x0, x_up, x_down, y_first.at[t], y_second.at[t], x_sem.at[t]

    def compute(t, g):
        for yy in range(4):
            for p in (0, 1):
                arrive(g, p, y0 + yy, 1 - k0)
        group = g % 4
        y_ref = y.at[t]

        def step(i, carry):
            lanes = pl.ds(pl.multiple_of(i * KSTEP, KSTEP), KSTEP)
            block = panels[group, :, :, :, :, lanes].reshape(2, 16, 8, KSTEP)
            block = (block * mask[:, :, lanes][:, None]).reshape(256, KSTEP)
            ph, plo = split(block)
            kh, kl = k_hi[:, lanes], k_lo[:, lanes]
            dims = (((1,), (1,)), ((), ()))
            g2 = functools.partial(lax.dot_general, dimension_numbers=dims, preferred_element_type=F32)
            total = (g2(kh, ph) + g2(kl, ph) + g2(kh, plo)).reshape(2, 4, 80, 256)

            @pl.when(i == 0)
            def _():
                y_ref[...] = total

            @pl.when(i > 0)
            def _():
                y_ref[...] += total

            return carry

        lax.fori_loop(0, 2560 // KSTEP, step, 0)
        ring_start(*x_ring(t))
        def hand(i):
            target = to_col(i)
            first_row = (((y_to % 2) * 2 + k0) * 8 + target) * 80
            start = jnp.minimum(first_row // BLK, 2560 // BLK - 2) * BLK
            lanes = pl.ds(pl.multiple_of(start, BLK), 256)
            window = panels[group, :, :, :, :, lanes].reshape(2, 16, 8, 256)
            window = (window * mask[:, :, lanes][:, None]).reshape(256, 256)
            turned[t, i] = window.T
            piece = turned.at[t, i, pl.ds(pl.multiple_of(first_row - start, 8), 80)]
            same = jnp.logical_and(to_row == row, target == col)

            @pl.when(same)
            def _():
                copy = pltpu.make_async_copy(piece, pieces.at[group], local_sem.at[3])
                copy.start()
                copy.wait()

            @pl.when(jnp.logical_not(same))
            def _():
                pltpu.make_async_remote_copy(
                    src_ref=piece, dst_ref=pieces.at[group], send_sem=p_send.at[t, i], recv_sem=p_recv.at[group],
                    device_id=(to_row, target), device_id_type=MESH,
                ).start()

        def hand_all():
            @pl.when(hands_out)
            def _():
                for i in range(4):
                    hand(i)

        if t < 3:
            hand_all()
        return hand_all

    def reduce_x(t):
        ring_wait(y_second.at[t], x_sem.at[t])

        def total(z):
            return y[t, z, x0] + y_second[t, 0, z] + y_second[t, 1, z]

        half_out[t] = total(1 - z0)
        send(half_out.at[t], half_in.at[t], z_sem.at[t], z_mate)
        own[t] = total(z0)

    def finish_y(t, g):
        landed(half_in.at[t], z_sem.at[t])
        done = own[t] + half_in[t]
        lanes = pl.ds(pl.multiple_of((g % 4) * BLK, BLK), BLK)
        blocks[0, :, lanes] = -done[:, :BLK]
        y_two[:, lanes] = done[:, BLK:]

    order = (g0, g0 + 1, g0 + 3, g0 + 2)

    for p in (0, 1):
        push(g0, p, y0, k0, y_up)
        push(g0, 1 - p, y0, k0, y_down)
        push(g0, p, y0, k0, g_up)
        push(g0, 1 - p, y0, k0, g_down)
        push(g0, p, y0, k0, sibling)
    k_copy.start()
    for copy in squares:
        copy.start()

    for p, present in ((0, present_one), (1, present_two)):
        for j in range(2560 // BLK):
            value = present[col * (2560 // BLK) + j].astype(F32)
            mask[p, :, j * BLK:(j + 1) * BLK] = jnp.full((8, BLK), value, F32)
    k_copy.wait()

    def split_rows(i, carry):
        rows = pl.ds(pl.multiple_of(i * 32, 32), 32)
        hi, lo = split(k_f32[rows, :])
        k_hi[rows, :] = hi
        k_lo[rows, :] = lo
        return carry

    lax.fori_loop(0, 20, split_rows, 0)

    relay_y(order[0])
    arrive(g0 + 3, 0, y0, k0)
    push(g0 + 3, 0, y0, k0, g_up)
    arrive(g0 + 1, 1, y0, k0)
    push(g0 + 1, 1, y0, k0, g_down)
    end_y(order[0])
    arrive(g0 + 1, 0, y0, k0)
    spread_y(order[1])
    compute(0, order[0])
    for copy in squares:
        copy.wait()
    hi, lo = split(coupling[...])
    c_split[0] = hi
    c_split[1] = lo
    pair = pl.ds(pl.multiple_of((col // 2) * BLK, BLK), BLK)
    for i, ref in enumerate((coupling, diag_one, diag_two)):
        slices[i] = ref[:, pair].T
    mine = pl.ds(pl.multiple_of((col % 2) * 64, 64), 64)
    relay_y(order[1])
    arrive(g0 + 3, 1, y0, k0)
    spread_y(order[2])
    ring_middle(*x_ring(0))
    end_y(order[1])
    compute(1, order[1])
    reduce_x(0)
    relay_y(order[2])
    arrive(g0 + 2, 0, y0, k0)
    arrive(g0 + 2, 1, y0, k0)
    spread_y(order[3])
    ring_middle(*x_ring(1))
    end_y(order[2])
    compute(2, order[2])
    reduce_x(1)
    finish_y(0, order[0])
    relay_y(order[3])
    ring_middle(*x_ring(2))
    diag_coupled = dot3(slices[0, mine, :], diag_one[...], ((1,), (1,)))
    end_y(order[3])
    hand_last = compute(3, order[3])
    reduce_x(2)
    finish_y(1, order[1])
    ring_middle(*x_ring(3))
    hand_last()
    finish_y(2, order[2])
    reduce_x(3)
    @pl.when(jnp.logical_not(stays))
    def _():
        for g in range(4):
            landed(pieces.at[g], p_recv.at[g])

    send(pieces.at[pl.ds(2 * (1 - k0), 2)], mate_pieces, mate_sem.at[1], sibling)
    finish_y(3, order[3])

    def times_coupling(left):
        lh, ll = split(left)
        g = functools.partial(jnp.dot, preferred_element_type=F32)
        return g(lh, c_split[0]) + (g(lh, c_split[1]) + g(ll, c_split[0]))

    send(blocks.at[0], mate_blocks.at[0], mate_sem.at[0], sibling)
    blocks[1] = -(y_two[...] + times_coupling(blocks[0]))
    send(blocks.at[1], mate_blocks.at[1], mate_sem.at[2], sibling)

    x1_out[...] = blocks[0]
    x2_out[...] = blocks[1]
    landed(mate_pieces, mate_sem.at[1])
    landed(mate_blocks.at[0], mate_sem.at[0])

    right = jnp.concatenate(
        [
            jnp.concatenate([pieces[2 * k0], pieces[2 * k0 + 1]], axis=1),
            jnp.concatenate([mate_pieces[0], mate_pieces[1]], axis=1),
        ],
        axis=0,
    )
    both = jnp.concatenate([right[:, 0:128], right[:, 256:384], right[:, 128:256], right[:, 384:512]], axis=1)
    both_hi, both_lo = split(both)

    def turned_times(i, width):
        left = jnp.concatenate([blocks[i].T, mate_blocks[i].T], axis=1)
        lh, ll = split(left)
        g = functools.partial(jnp.dot, preferred_element_type=F32)
        rh, rl = both_hi[:, :width], both_lo[:, :width]
        return g(lh, rh) + (g(lh, rl) + g(ll, rh))

    def place(sums, j, value):
        value = value.reshape(2, 4, 4, 16, 256)
        for z in (0, 1):
            for w in range(4):
                sums[0, w, z, :, j] = value[z, w, :, :, :BLK]
                sums[1, w, z, :, j] = value[z, :, w, :, BLK:]

    ring_x, ring_y = (x0, x_up, x_down), (y0, y_up, y_down)
    steps = ((sums_a, a_first, a_second), (sums_b, b_first, b_second))

    def whole(i, side):
        sums, first, second = steps[i]
        ring = (ring_x, ring_y)[side]
        return (lambda w, z: sums.at[side, w, z]), *ring, first.at[side], second.at[side], sum_sem.at[i, side]

    place(sums_a, 0, turned_times(0, 256))
    for side in (0, 1):
        ring_start(*whole(0, side))
    landed(mate_blocks.at[1], mate_sem.at[2])
    later = turned_times(1, 512)
    place(sums_b, 0, later[:, :256])
    place(sums_b, 1, later[:, 256:])
    for side in (0, 1):
        ring_start(*whole(1, side))
    part_of = [
        ((lambda w, z, side=side: rest.at[side, w, z]), *ring, r_first.at[side], r_second.at[side], rest_sem.at[side])
        for side, ring in ((0, ring_y), (1, ring_x))
    ]
    for i in (0, 1):
        for side in (0, 1):
            ring_middle(*whole(i, side))
    for side in (0, 1):
        me = (x0, y0)[side]
        for i, (sums, first, second) in enumerate(steps):
            ring_wait(second.at[side], sum_sem.at[i, side])
            for z in (0, 1):
                rest[side, :, z, i:2 * i + 1] = sums[side, me, z] + second[side, 0, z] + second[side, 1, z]
        ring_start(*part_of[side])
    for side in (0, 1):
        ring_middle(*part_of[side])
    for side in (0, 1):
        ring_wait(r_second.at[side], rest_sem.at[side])
        me = (y0, x0)[side]
        for z in (0, 1):
            z_pair[z, side] = rest[side, me, z] + r_second[side, 0, z] + r_second[side, 1, z]
    send(z_pair.at[1 - z0], z_in, tail_sem.at[0], z_mate)
    landed(z_in, tail_sem.at[0])
    over_g[...] = z_pair[z0] + z_in[...]
    for d, device in enumerate((g_up, g_down, g_far)):
        send(over_g, g_in.at[d], tail_sem.at[1 + d], device)
    for d in range(3):
        landed(g_in.at[d], tail_sem.at[1 + d])
    even = over_g[...] + g_in[2]
    odd = g_in[0] + g_in[1]
    gathered[k0, y0] = even + odd
    mine_ref = gathered.at[k0, y0]
    for device in (y_up, y_down, y_far, sibling):
        send(mine_ref, mine_ref, end_sem.at[k0, y0], device)
    for d in (1, 3, 2):
        ref = gathered.at[k0, (y0 + d) % 4]
        landed(ref, end_sem.at[k0, (y0 + d) % 4])
        send(ref, ref, end_sem.at[k0, (y0 + d) % 4], sibling)
    for d in range(4):
        ref = gathered.at[1 - k0, (y0 + d) % 4]
        landed(ref, end_sem.at[1 - k0, (y0 + d) % 4])

    def total_of(j):
        return jnp.concatenate(
            [
                jnp.concatenate([gathered[k, w, side, j] for w in range(4)], axis=0)
                for k in (0, 1)
                for side in (0, 1)
            ],
            axis=1,
        )

    first_out[...] = slices[1, mine, :] - total_of(0)
    cross = -total_of(1) - diag_coupled
    cross_out[...] = cross
    second_out[...] = slices[2, mine, :] - total_of(2) - times_coupling(cross)
    send.finish()

    @pl.when(hands_out)
    def _():
        for i in range(4):
            @pl.when(jnp.logical_not(jnp.logical_and(to_row == row, to_col(i) == col)))
            def _():
                for t in range(4):
                    pltpu.make_async_remote_copy(
                        src_ref=turned.at[t, i, pl.ds(0, 80)], dst_ref=pieces.at[t], send_sem=p_send.at[t, i],
                        recv_sem=p_recv.at[t], device_id=giver, device_id_type=MESH,
                    ).wait_send()


def update(known_inverse, one, two, coupling, diag_one, diag_two, present_one, present_two):
    vmem = pl.BlockSpec(memory_space=pltpu.VMEM)
    hbm = pl.BlockSpec(memory_space=pl.ANY)
    smem = pl.BlockSpec(memory_space=pltpu.SMEM)
    dma = pltpu.SemaphoreType.DMA
    tall = jax.ShapeDtypeStruct((80, 512), F32)
    small = jax.ShapeDtypeStruct((64, 512), F32)
    return pl.pallas_call(
        update_kernel,
        out_shape=(tall, tall, small, small, small),
        in_specs=[hbm] * 6 + [smem, smem],
        out_specs=(vmem,) * 5,
        scratch_shapes=[
            pltpu.VMEM((512, 512), F32),
            pltpu.VMEM((512, 512), F32),
            pltpu.VMEM((512, 512), F32),
            pltpu.VMEM((640, 2560), F32),
            pltpu.VMEM((640, 2560), BF16),
            pltpu.VMEM((640, 2560), BF16),
            pltpu.VMEM((4, 2, 4, 2, 16, 2560), F32),
            pltpu.VMEM((2, 8, 2560), F32),
            pltpu.VMEM((4, 2, 4, 80, 256), F32),
            pltpu.VMEM((4, 2, 80, 256), F32),
            pltpu.VMEM((4, 2, 2, 80, 256), F32),
            pltpu.VMEM((4, 80, 256), F32),
            pltpu.VMEM((4, 80, 256), F32),
            pltpu.VMEM((4, 80, 256), F32),
            pltpu.VMEM((4, 4, 256, 256), F32),
            pltpu.VMEM((80, 512), F32),
            pltpu.VMEM((4, 80, 256), F32),
            pltpu.VMEM((2, 80, 256), F32),
            pltpu.VMEM((2, 80, 512), F32),
            pltpu.VMEM((2, 80, 512), F32),
            pltpu.VMEM((3, 128, 512), F32),
            pltpu.VMEM((2, 512, 512), BF16),
            pltpu.VMEM((2, 4, 2, 4, 1, 16, 128), F32),
            pltpu.VMEM((2, 2, 4, 1, 16, 128), F32),
            pltpu.VMEM((2, 2, 2, 4, 1, 16, 128), F32),
            pltpu.VMEM((2, 4, 2, 4, 2, 16, 128), F32),
            pltpu.VMEM((2, 2, 4, 2, 16, 128), F32),
            pltpu.VMEM((2, 2, 2, 4, 2, 16, 128), F32),
            pltpu.VMEM((2, 4, 2, 3, 16, 128), F32),
            pltpu.VMEM((2, 2, 3, 16, 128), F32),
            pltpu.VMEM((2, 2, 2, 3, 16, 128), F32),
            pltpu.VMEM((2, 2, 3, 16, 128), F32),
            pltpu.VMEM((2, 3, 16, 128), F32),
            pltpu.VMEM((2, 3, 16, 128), F32),
            pltpu.VMEM((3, 2, 3, 16, 128), F32),
            pltpu.VMEM((2, 4, 2, 3, 16, 128), F32),
            dma((7,)),
            dma((160,)),
            dma((4, 2, 4, 2)),
            dma((4, 6)),
            dma((4,)),
            dma((4, 4)),
            dma((4,)),
            dma((3,)),
            dma((2, 2, 6)),
            dma((2, 6)),
            dma((4,)),
            dma((2, 4)),
        ],
        compiler_params=pltpu.CompilerParams(
            collective_id=0, has_side_effects=True, vmem_limit_bytes=56 * 2**20
        ),
        name="update",
    )(known_inverse, one, two, coupling, diag_one, diag_two, present_one, present_two)


def emit_kernel(*refs):
    for source, target in zip(refs[:5], refs[5:]):
        target[...] = source[...]


def emit(*arrays):
    vmem = pl.BlockSpec(memory_space=pltpu.VMEM)
    return pl.pallas_call(
        emit_kernel,
        out_shape=tuple(jax.ShapeDtypeStruct(a.shape, a.dtype) for a in arrays),
        in_specs=[vmem] * 5,
        out_specs=(vmem,) * 5,
        name="emit",
    )(*arrays)


def on_device(known_inverse, first_panel, second_panel, coupling, first_diag, second_diag, first_present, second_present):
    x1, x2, first, cross, second = emit(
        *update(
            known_inverse, first_panel.T, second_panel.T, coupling, first_diag, second_diag, first_present, second_present
        )
    )
    return x1, first.T, x2, cross.T, second.T


def solution(mesh):
    in_specs = (P("row", "col"), P("col", "row"), P("col", "row"), P(), P(), P(), P(), P())
    out_specs = (P(("row", "col"), None), P(None, "col"), P(("row", "col"), None), P(None, "col"), P(None, "col"))
    return jax.shard_map(on_device, mesh=mesh, in_specs=in_specs, out_specs=out_specs, check_vma=False)
```

```python
import functools

import jax
import jax.numpy as jnp
from jax import lax
from jax.experimental import pallas as pl
from jax.experimental.pallas import tpu as pltpu
from jax.sharding import PartitionSpec as P

BLK = 128
MESH = pl.DeviceIdType.MESH
F32 = jnp.float32
BF16 = jnp.bfloat16
KSTEP = 512


def split(x):
    hi = x.astype(BF16)
    return hi, (x - hi.astype(F32)).astype(BF16)


def dot3(left, right, dims):
    lh, ll = split(left)
    rh, rl = split(right)
    g = functools.partial(lax.dot_general, dimension_numbers=(dims, ((), ())), preferred_element_type=F32)
    return g(lh, rh) + (g(lh, rl) + g(ll, rh))


class Sends:
    def __init__(self, sems):
        self.sems = sems
        self.started = []

    def __call__(self, src, dst, recv, device):
        copy = pltpu.make_async_remote_copy(
            src_ref=src, dst_ref=dst, send_sem=self.sems.at[len(self.started)], recv_sem=recv,
            device_id=device, device_id_type=MESH,
        )
        copy.start()
        self.started.append(copy)
        return copy

    def finish(self):
        for copy in self.started:
            copy.wait_send()


def update_kernel(
    k_hbm, one_hbm, two_hbm, c_hbm, d_one_hbm, d_two_hbm, present_one, present_two,
    x1_out, x2_out, first_out, cross_out, second_out,
    coupling, diag_one, diag_two,
    k_f32, k_hi, k_lo, panels, mask, y, y_first, y_second, half_out, half_in, own, turned, y_two,
    pieces, mate_pieces, blocks, mate_blocks, slices, c_split, sums_a, a_first, a_second, sums_b, b_first, b_second, rest, r_in,
    z_pair, z_in, over_g, g_in, gathered,
    local_sem, send_sem, recv_sem, x_sem, z_sem, p_send, p_recv, mate_sem, sum_sem, rest_sem, tail_sem, end_sem,
):
    row = lax.axis_index("row")
    col = lax.axis_index("col")
    g0, y0, k0 = row // 8, (row // 2) % 4, row % 2
    z0, x0 = col // 4, col % 4

    def at(g, yy, k):
        return ((g % 4) * 8 + (yy % 4) * 2 + k, col)

    y_up, y_down = at(g0, y0 + 1, k0), at(g0, y0 + 3, k0)
    g_up, g_down = at(g0 + 1, y0, k0), at(g0 + 3, y0, k0)
    sibling = at(g0, y0, 1 - k0)
    x_up, x_down = (row, z0 * 4 + (x0 + 1) % 4), (row, z0 * 4 + (x0 + 3) % 4)
    y_far, g_far = at(g0, y0 + 2, k0), at(g0 + 2, y0, k0)
    x_far = (row, z0 * 4 + (x0 + 2) % 4)
    z_mate = (row, (1 - z0) * 4 + x0)
    hands_out = g0 == col // 2
    level = (y0 // 2) == (col % 2)
    y_to = jnp.where(level, y0, 3 - y0)
    to_row = g0 * 8 + y_to * 2 + k0
    x_first = x0 + jnp.where(level, 0, 2)

    def to_col(i):
        return (i // 2) * 4 + (x_first + i % 2) % 4

    giver_col = row // 4
    y_from = jnp.where((x0 - giver_col % 4 + 4) % 4 < 2, y0, 3 - y0)
    giver = (g0 * 8 + y_from * 2 + k0, giver_col)
    stays = jnp.logical_and(giver[0] == row, giver_col == col)

    k_copy = pltpu.make_async_copy(k_hbm, k_f32, local_sem.at[0])
    firsts = [
        pltpu.make_async_copy(one_hbm, panels.at[g0, 0, y0, k0], local_sem.at[1]),
        pltpu.make_async_copy(two_hbm, panels.at[g0, 1, y0, k0], local_sem.at[2]),
    ]
    for copy in firsts:
        copy.start()

    barrier = pltpu.get_barrier_semaphore()
    for device in (y_up, y_down, y_far, g_up, g_down, g_far, sibling, x_up, x_down, x_far, z_mate):
        pl.semaphore_signal(barrier, inc=1, device_id=device, device_id_type=MESH)

    @pl.when(hands_out)
    def _():
        for i in range(4):
            @pl.when(jnp.logical_not(jnp.logical_and(to_row == row, to_col(i) == col)))
            def _():
                pl.semaphore_signal(barrier, inc=1, device_id=(to_row, to_col(i)), device_id_type=MESH)

    @pl.when(jnp.logical_not(stays))
    def _():
        pl.semaphore_signal(barrier, inc=1, device_id=giver, device_id_type=MESH)

    extra = jnp.where(hands_out, 4, 0) + jnp.where(stays, -1, 1)
    pl.semaphore_wait(barrier, 11 + extra)
    for copy in firsts:
        copy.wait()
    squares = [
        pltpu.make_async_copy(source, target, local_sem.at[i])
        for i, source, target in ((4, c_hbm, coupling), (5, d_one_hbm, diag_one), (6, d_two_hbm, diag_two))
    ]

    send = Sends(send_sem)

    def landed(ref, sem):
        pltpu.make_async_remote_copy(
            src_ref=ref, dst_ref=ref, send_sem=send_sem.at[0], recv_sem=sem, device_id=sibling, device_id_type=MESH
        ).wait_recv()

    def ring_start(src, me, up, down, first, second, sem):
        send(src((me + 2) % 4, 0), first.at[0], sem.at[0], up)
        send(src((me + 2) % 4, 1), first.at[1], sem.at[1], down)
        send(src((me + 1) % 4, 1), second.at[0, 1], sem.at[3], up)
        send(src((me + 3) % 4, 0), second.at[1, 0], sem.at[4], down)

    def ring_middle(src, me, up, down, first, second, sem):
        landed(first.at[0], sem.at[0])
        src((me + 1) % 4, 0)[...] += first[0]
        send(src((me + 1) % 4, 0), second.at[0, 0], sem.at[2], up)
        landed(first.at[1], sem.at[1])
        src((me + 3) % 4, 1)[...] += first[1]
        send(src((me + 3) % 4, 1), second.at[1, 1], sem.at[5], down)

    def ring_wait(second, sem):
        for a in (0, 1):
            for b in (0, 1):
                landed(second.at[a, b], sem.at[2 + 2 * a + b])

    def part(g, p, yy, k):
        return panels.at[g % 4, p, yy % 4, k]

    def push(g, p, yy, k, device):
        ref = part(g, p, yy, k)
        send(ref, ref, recv_sem.at[g % 4, p, yy % 4, k], device)

    def arrive(g, p, yy, k):
        ref = part(g, p, yy, k)
        landed(ref, recv_sem.at[g % 4, p, yy % 4, k])

    def spread_y(g):
        for p in (0, 1):
            push(g, p, y0, k0, y_up)
            push(g, 1 - p, y0, k0, y_down)
        push(g, 0, y0, k0, sibling)
        push(g, 1, y0, k0, sibling)

    def relay_y(g):
        arrive(g, 0, y0 + 3, k0)
        push(g, 0, y0 + 3, k0, y_up)
        push(g, 0, y0 + 3, k0, sibling)
        arrive(g, 1, y0 + 1, k0)
        push(g, 1, y0 + 1, k0, y_down)
        push(g, 1, y0 + 1, k0, sibling)
        arrive(g, 1, y0 + 3, k0)
        push(g, 1, y0 + 3, k0, sibling)
        arrive(g, 0, y0 + 1, k0)
        push(g, 0, y0 + 1, k0, sibling)

    def end_y(g):
        for p in (0, 1):
            arrive(g, p, y0 + 2, k0)
            push(g, p, y0 + 2, k0, sibling)

    def x_ring(t):
        return (lambda x, z: y.at[t, z, x]), x0, x_up, x_down, y_first.at[t], y_second.at[t], x_sem.at[t]

    def compute(t, g):
        for yy in range(4):
            for p in (0, 1):
                arrive(g, p, y0 + yy, 1 - k0)
        group = g % 4
        y_ref = y.at[t]

        def step(i, carry):
            lanes = pl.ds(pl.multiple_of(i * KSTEP, KSTEP), KSTEP)
            block = panels[group, :, :, :, :, lanes].reshape(2, 16, 8, KSTEP)
            block = (block * mask[:, :, lanes][:, None]).reshape(256, KSTEP)
            ph, plo = split(block)
            kh, kl = k_hi[:, lanes], k_lo[:, lanes]
            dims = (((1,), (1,)), ((), ()))
            g2 = functools.partial(lax.dot_general, dimension_numbers=dims, preferred_element_type=F32)
            total = (g2(kh, ph) + g2(kl, ph) + g2(kh, plo)).reshape(2, 4, 80, 256)

            @pl.when(i == 0)
            def _():
                y_ref[...] = total

            @pl.when(i > 0)
            def _():
                y_ref[...] += total

            return carry

        lax.fori_loop(0, 2560 // KSTEP, step, 0)
        ring_start(*x_ring(t))
        def hand(i):
            target = to_col(i)
            first_row = (((y_to % 2) * 2 + k0) * 8 + target) * 80
            start = jnp.minimum(first_row // BLK, 2560 // BLK - 2) * BLK
            lanes = pl.ds(pl.multiple_of(start, BLK), 256)
            window = panels[group, :, :, :, :, lanes].reshape(2, 16, 8, 256)
            window = (window * mask[:, :, lanes][:, None]).reshape(256, 256)
            turned[t, i] = window.T
            piece = turned.at[t, i, pl.ds(pl.multiple_of(first_row - start, 8), 80)]
            same = jnp.logical_and(to_row == row, target == col)

            @pl.when(same)
            def _():
                copy = pltpu.make_async_copy(piece, pieces.at[group], local_sem.at[3])
                copy.start()
                copy.wait()

            @pl.when(jnp.logical_not(same))
            def _():
                pltpu.make_async_remote_copy(
                    src_ref=piece, dst_ref=pieces.at[group], send_sem=p_send.at[t, i], recv_sem=p_recv.at[group],
                    device_id=(to_row, target), device_id_type=MESH,
                ).start()

        def hand_all():
            @pl.when(hands_out)
            def _():
                for i in range(4):
                    hand(i)

        return hand_all

    def reduce_x(t):
        ring_wait(y_second.at[t], x_sem.at[t])

        def total(z):
            return y[t, z, x0] + y_second[t, 0, z] + y_second[t, 1, z]

        half_out[t] = total(1 - z0)
        send(half_out.at[t], half_in.at[t], z_sem.at[t], z_mate)
        own[t] = total(z0)

    def finish_y(t, g):
        landed(half_in.at[t], z_sem.at[t])
        done = own[t] + half_in[t]
        lanes = pl.ds(pl.multiple_of((g % 4) * BLK, BLK), BLK)
        blocks[0, :, lanes] = -done[:, :BLK]
        y_two[:, lanes] = done[:, BLK:]

    order = (g0, g0 + 1, g0 + 3, g0 + 2)

    for p in (0, 1):
        push(g0, p, y0, k0, y_up)
        push(g0, 1 - p, y0, k0, y_down)
        push(g0, p, y0, k0, g_up)
        push(g0, 1 - p, y0, k0, g_down)
        push(g0, p, y0, k0, sibling)
    k_copy.start()
    for copy in squares:
        copy.start()

    for p, present in ((0, present_one), (1, present_two)):
        for j in range(2560 // BLK):
            value = present[col * (2560 // BLK) + j].astype(F32)
            mask[p, :, j * BLK:(j + 1) * BLK] = jnp.full((8, BLK), value, F32)
    k_copy.wait()

    def split_rows(i, carry):
        rows = pl.ds(pl.multiple_of(i * 32, 32), 32)
        hi, lo = split(k_f32[rows, :])
        k_hi[rows, :] = hi
        k_lo[rows, :] = lo
        return carry

    lax.fori_loop(0, 20, split_rows, 0)

    relay_y(order[0])
    arrive(g0 + 3, 0, y0, k0)
    push(g0 + 3, 0, y0, k0, g_up)
    arrive(g0 + 1, 1, y0, k0)
    push(g0 + 1, 1, y0, k0, g_down)
    end_y(order[0])
    arrive(g0 + 1, 0, y0, k0)
    spread_y(order[1])
    hand_0 = compute(0, order[0])
    for copy in squares:
        copy.wait()
    hi, lo = split(coupling[...])
    c_split[0] = hi
    c_split[1] = lo
    pair = pl.ds(pl.multiple_of((col // 2) * BLK, BLK), BLK)
    for i, ref in enumerate((coupling, diag_one, diag_two)):
        slices[i] = ref[:, pair].T
    mine = pl.ds(pl.multiple_of((col % 2) * 64, 64), 64)
    relay_y(order[1])
    arrive(g0 + 3, 1, y0, k0)
    spread_y(order[2])
    ring_middle(*x_ring(0))
    end_y(order[1])
    hand_1 = compute(1, order[1])
    reduce_x(0)
    relay_y(order[2])
    arrive(g0 + 2, 0, y0, k0)
    arrive(g0 + 2, 1, y0, k0)
    spread_y(order[3])
    ring_middle(*x_ring(1))
    hand_0()
    end_y(order[2])
    hand_2 = compute(2, order[2])
    reduce_x(1)
    finish_y(0, order[0])
    relay_y(order[3])
    ring_middle(*x_ring(2))
    hand_1()
    hand_2()
    diag_coupled = dot3(slices[0, mine, :], diag_one[...], ((1,), (1,)))
    end_y(order[3])
    hand_last = compute(3, order[3])
    reduce_x(2)
    finish_y(1, order[1])
    ring_middle(*x_ring(3))
    hand_last()
    finish_y(2, order[2])
    reduce_x(3)
    @pl.when(jnp.logical_not(stays))
    def _():
        for g in range(4):
            landed(pieces.at[g], p_recv.at[g])

    send(pieces.at[pl.ds(2 * (1 - k0), 2)], mate_pieces, mate_sem.at[1], sibling)
    finish_y(3, order[3])

    def times_coupling(left):
        lh, ll = split(left)
        g = functools.partial(jnp.dot, preferred_element_type=F32)
        return g(lh, c_split[0]) + (g(lh, c_split[1]) + g(ll, c_split[0]))

    send(blocks.at[0], mate_blocks.at[0], mate_sem.at[0], sibling)
    blocks[1] = -(y_two[...] + times_coupling(blocks[0]))
    send(blocks.at[1], mate_blocks.at[1], mate_sem.at[2], sibling)

    x1_out[...] = blocks[0]
    x2_out[...] = blocks[1]
    landed(mate_pieces, mate_sem.at[1])
    landed(mate_blocks.at[0], mate_sem.at[0])

    right = jnp.concatenate(
        [
            jnp.concatenate([pieces[2 * k0], pieces[2 * k0 + 1]], axis=1),
            jnp.concatenate([mate_pieces[0], mate_pieces[1]], axis=1),
        ],
        axis=0,
    )
    both = jnp.concatenate([right[:, 0:128], right[:, 256:384], right[:, 128:256], right[:, 384:512]], axis=1)
    both_hi, both_lo = split(both)

    def turned_times(i, width):
        left = jnp.concatenate([blocks[i].T, mate_blocks[i].T], axis=1)
        lh, ll = split(left)
        g = functools.partial(jnp.dot, preferred_element_type=F32)
        rh, rl = both_hi[:, :width], both_lo[:, :width]
        return g(lh, rh) + (g(lh, rl) + g(ll, rh))

    def place(sums, j, value):
        value = value.reshape(2, 4, 4, 16, 256)
        for z in (0, 1):
            for w in range(4):
                sums[0, w, z, :, j] = value[z, w, :, :, :BLK]
                sums[1, w, z, :, j] = value[z, :, w, :, BLK:]

    ring_x, ring_y = (x0, x_up, x_down), (y0, y_up, y_down)
    steps = ((sums_a, a_first, a_second), (sums_b, b_first, b_second))

    def whole(i, side):
        sums, first, second = steps[i]
        ring = (ring_x, ring_y)[side]
        return (lambda w, z: sums.at[side, w, z]), *ring, first.at[side], second.at[side], sum_sem.at[i, side]

    place(sums_a, 0, turned_times(0, 256))
    for side in (0, 1):
        ring_start(*whole(0, side))
    landed(mate_blocks.at[1], mate_sem.at[2])
    later = turned_times(1, 512)
    place(sums_b, 0, later[:, :256])
    place(sums_b, 1, later[:, 256:])
    for side in (0, 1):
        ring_start(*whole(1, side))
    mates = ((y_up, y_far, y_down), (x_up, x_far, x_down))
    for i in (0, 1):
        for side in (0, 1):
            ring_middle(*whole(i, side))
    for side in (0, 1):
        me = (x0, y0)[side]
        for i, (sums, first, second) in enumerate(steps):
            ring_wait(second.at[side], sum_sem.at[i, side])
            for z in (0, 1):
                rest[side, :, z, i:2 * i + 1] = sums[side, me, z] + second[side, 0, z] + second[side, 1, z]
        other = (y0, x0)[side]
        for d in (2, 1, 3):
            send(rest.at[side, (other + d) % 4], r_in.at[side, d - 1], rest_sem.at[side, d - 1], mates[side][d - 1])
    for side in (0, 1):
        me = (y0, x0)[side]
        for d in range(3):
            landed(r_in.at[side, d], rest_sem.at[side, d])
        for z in (0, 1):
            z_pair[z, side] = (rest[side, me, z] + r_in[side, 0, z]) + (r_in[side, 1, z] + r_in[side, 2, z])
    send(z_pair.at[1 - z0], z_in, tail_sem.at[0], z_mate)
    landed(z_in, tail_sem.at[0])
    over_g[...] = z_pair[z0] + z_in[...]
    for d, device in enumerate((g_up, g_down, g_far)):
        send(over_g, g_in.at[d], tail_sem.at[1 + d], device)
    for d in range(3):
        landed(g_in.at[d], tail_sem.at[1 + d])
    even = over_g[...] + g_in[2]
    odd = g_in[0] + g_in[1]
    gathered[k0, y0] = even + odd
    mine_ref = gathered.at[k0, y0]
    for device in (y_up, y_down, y_far, sibling):
        send(mine_ref, mine_ref, end_sem.at[k0, y0], device)
    for d in (1, 3, 2):
        ref = gathered.at[k0, (y0 + d) % 4]
        landed(ref, end_sem.at[k0, (y0 + d) % 4])
        send(ref, ref, end_sem.at[k0, (y0 + d) % 4], sibling)
    for d in range(4):
        ref = gathered.at[1 - k0, (y0 + d) % 4]
        landed(ref, end_sem.at[1 - k0, (y0 + d) % 4])

    def total_of(j):
        return jnp.concatenate(
            [
                jnp.concatenate([gathered[k, w, side, j] for w in range(4)], axis=0)
                for k in (0, 1)
                for side in (0, 1)
            ],
            axis=1,
        )

    first_out[...] = slices[1, mine, :] - total_of(0)
    cross = -total_of(1) - diag_coupled
    cross_out[...] = cross
    second_out[...] = slices[2, mine, :] - total_of(2) - times_coupling(cross)
    send.finish()

    @pl.when(hands_out)
    def _():
        for i in range(4):
            @pl.when(jnp.logical_not(jnp.logical_and(to_row == row, to_col(i) == col)))
            def _():
                for t in range(4):
                    pltpu.make_async_remote_copy(
                        src_ref=turned.at[t, i, pl.ds(0, 80)], dst_ref=pieces.at[t], send_sem=p_send.at[t, i],
                        recv_sem=p_recv.at[t], device_id=giver, device_id_type=MESH,
                    ).wait_send()


def update(known_inverse, one, two, coupling, diag_one, diag_two, present_one, present_two):
    vmem = pl.BlockSpec(memory_space=pltpu.VMEM)
    hbm = pl.BlockSpec(memory_space=pl.ANY)
    smem = pl.BlockSpec(memory_space=pltpu.SMEM)
    dma = pltpu.SemaphoreType.DMA
    tall = jax.ShapeDtypeStruct((80, 512), F32)
    small = jax.ShapeDtypeStruct((64, 512), F32)
    return pl.pallas_call(
        update_kernel,
        out_shape=(tall, tall, small, small, small),
        in_specs=[hbm] * 6 + [smem, smem],
        out_specs=(vmem,) * 5,
        scratch_shapes=[
            pltpu.VMEM((512, 512), F32),
            pltpu.VMEM((512, 512), F32),
            pltpu.VMEM((512, 512), F32),
            pltpu.VMEM((640, 2560), F32),
            pltpu.VMEM((640, 2560), BF16),
            pltpu.VMEM((640, 2560), BF16),
            pltpu.VMEM((4, 2, 4, 2, 16, 2560), F32),
            pltpu.VMEM((2, 8, 2560), F32),
            pltpu.VMEM((4, 2, 4, 80, 256), F32),
            pltpu.VMEM((4, 2, 80, 256), F32),
            pltpu.VMEM((4, 2, 2, 80, 256), F32),
            pltpu.VMEM((4, 80, 256), F32),
            pltpu.VMEM((4, 80, 256), F32),
            pltpu.VMEM((4, 80, 256), F32),
            pltpu.VMEM((4, 4, 256, 256), F32),
            pltpu.VMEM((80, 512), F32),
            pltpu.VMEM((4, 80, 256), F32),
            pltpu.VMEM((2, 80, 256), F32),
            pltpu.VMEM((2, 80, 512), F32),
            pltpu.VMEM((2, 80, 512), F32),
            pltpu.VMEM((3, 128, 512), F32),
            pltpu.VMEM((2, 512, 512), BF16),
            pltpu.VMEM((2, 4, 2, 4, 1, 16, 128), F32),
            pltpu.VMEM((2, 2, 4, 1, 16, 128), F32),
            pltpu.VMEM((2, 2, 2, 4, 1, 16, 128), F32),
            pltpu.VMEM((2, 4, 2, 4, 2, 16, 128), F32),
            pltpu.VMEM((2, 2, 4, 2, 16, 128), F32),
            pltpu.VMEM((2, 2, 2, 4, 2, 16, 128), F32),
            pltpu.VMEM((2, 4, 2, 3, 16, 128), F32),
            pltpu.VMEM((2, 3, 2, 3, 16, 128), F32),
            pltpu.VMEM((2, 2, 3, 16, 128), F32),
            pltpu.VMEM((2, 3, 16, 128), F32),
            pltpu.VMEM((2, 3, 16, 128), F32),
            pltpu.VMEM((3, 2, 3, 16, 128), F32),
            pltpu.VMEM((2, 4, 2, 3, 16, 128), F32),
            dma((7,)),
            dma((160,)),
            dma((4, 2, 4, 2)),
            dma((4, 6)),
            dma((4,)),
            dma((4, 4)),
            dma((4,)),
            dma((3,)),
            dma((2, 2, 6)),
            dma((2, 6)),
            dma((4,)),
            dma((2, 4)),
        ],
        compiler_params=pltpu.CompilerParams(
            collective_id=0, has_side_effects=True, vmem_limit_bytes=56 * 2**20
        ),
        name="update",
    )(known_inverse, one, two, coupling, diag_one, diag_two, present_one, present_two)


def emit_kernel(*refs):
    for source, target in zip(refs[:5], refs[5:]):
        target[...] = source[...]


def emit(*arrays):
    vmem = pl.BlockSpec(memory_space=pltpu.VMEM)
    return pl.pallas_call(
        emit_kernel,
        out_shape=tuple(jax.ShapeDtypeStruct(a.shape, a.dtype) for a in arrays),
        in_specs=[vmem] * 5,
        out_specs=(vmem,) * 5,
        name="emit",
    )(*arrays)


def on_device(known_inverse, first_panel, second_panel, coupling, first_diag, second_diag, first_present, second_present):
    x1, x2, first, cross, second = emit(
        *update(
            known_inverse, first_panel.T, second_panel.T, coupling, first_diag, second_diag, first_present, second_present
        )
    )
    return x1, first.T, x2, cross.T, second.T


def solution(mesh):
    in_specs = (P("row", "col"), P("col", "row"), P("col", "row"), P(), P(), P(), P(), P())
    out_specs = (P(("row", "col"), None), P(None, "col"), P(("row", "col"), None), P(None, "col"), P(None, "col"))
    return jax.shard_map(on_device, mesh=mesh, in_specs=in_specs, out_specs=out_specs, check_vma=False)
```
